512 devices in a mesh: pt: 64 (over z_hi, x, y), sub: 8 (over z_lo, core).
Axes of the slice: x: 4, y: 4, z: 16 (z_hi: 4, z_lo: 4; z = z_hi * 4 + z_lo), core: 2. Of those that a mesh axis runs over, the one named last changes fastest.
Arguments:
- kernel_diag: bfloat16 [131072, 256], P(('pt', 'sub')), may hold values from -1 to 4
- pair_quads: bfloat16 [2, 131072, 128], P(None, ('pt', 'sub')), may hold values from -0.21875 to 0.21875
- tile_mask: int32 [2, 1024, 1], P(None, ('pt', 'sub')), may hold values 0 or 1
- right_side: float32 [131072, 64], P(('pt', 'sub')), may hold values from -40 to 40
- basis: float32 [131072, 256], P(('pt', 'sub')), may hold values from -1 to 1
- spectrum: float32 [256], replicated, may hold values from 0.25 to 2
Outputs:
- solution: float32 [131072, 64], P(('pt', 'sub'))
- residual: float32 [131072, 64], P(('pt', 'sub'))
The draws below stay inside these ranges and needn't reach their ends.
All inputs are finite; a program needn't handle non-finite values. No bound on the sum of `tile_mask` on one device may be relied on, other than what follows from the above.
Results may differ from the reference program's by a relative error of at most 0.006.
Values may be sent and summed in bfloat16 or wider, within the bound.
A program may use at most 64 MiB of HBM per device.

```python
import math
import jax
import jax.numpy as jnp
from jax import lax

ROWS = 256
TILE = 128
RHS = 64
RANK = 256
ITERS = 2
HALF = 128
NPTS = 131072
N_PT = 64
N_SUB = 8


def shared_basis(key):
    entries = jnp.clip(jax.random.normal(jax.random.fold_in(key, 11), (NPTS, RANK), jnp.float32), -5.0, 5.0)
    return entries / math.sqrt(RANK)


def draw_basis(key, part):
    return shared_basis(key)


def draw_right_side(key, part):
    columns_basis = shared_basis(key)
    mixing = jnp.clip(jax.random.normal(jax.random.fold_in(key, 12), (RANK, RHS), jnp.float32), -4.0, 4.0)
    noise = jnp.clip(jax.random.normal(jax.random.fold_in(key, 13), (NPTS, RHS), jnp.float32), -5.0, 5.0)
    return noise + jnp.dot(columns_basis, mixing, precision=lax.Precision.HIGHEST)


def draw_kernel_diag(key, part):
    block_count = NPTS // ROWS
    entries = jnp.clip(jax.random.normal(jax.random.fold_in(key, 21), (block_count, ROWS, ROWS), jnp.float32), -5.0, 5.0)
    symmetric = (entries + jnp.swapaxes(entries, 1, 2)) / math.sqrt(2.0)
    blocks = 0.6 * symmetric / math.sqrt(ROWS) + 2.5 * jnp.eye(ROWS, dtype=jnp.float32)[None]
    return blocks.reshape(NPTS, ROWS).astype(jnp.bfloat16)


def with_ends(values, own_key, least, largest):
    spot = [jax.random.randint(jax.random.fold_in(own_key, axis), (), 0, length) for axis, length in enumerate(values.shape)]
    widest = values.shape.index(max(values.shape))
    next_to = spot[:widest] + [(spot[widest] + 1) % values.shape[widest]] + spot[widest + 1:]
    return values.at[tuple(spot)].set(least).at[tuple(next_to)].set(largest)


def block_scale(key, dims, split, smallest, high):
    def one(dim, blocks):
        heights = jax.random.uniform(jax.random.fold_in(jax.random.fold_in(key, 6), dim), (blocks,), jnp.float32, smallest / len(split), high / len(split))
        return jnp.repeat(jnp.exp(heights), dims[dim] // blocks).reshape((-1,) + (1,) * (len(dims) - dim - 1))

    level = one(*split[0])
    for cut in split[1:]:
        level = level * one(*cut)
    return level


def scatter_about(own_key, extent, spread, bound, pieces=(), kind=jnp.bfloat16):
    values = spread * jax.random.normal(own_key, extent, jnp.float32)
    if pieces:
        values = values * block_scale(own_key, extent, pieces, -0.22, 0.18)
    return jnp.clip(values, -bound, bound).astype(kind)


def setup_inputs(seed: int = 0) -> dict:
    splits = jax.random.split(jax.random.key(seed), 7)
    return {
        "kernel_diag": draw_kernel_diag(jax.random.fold_in(splits[6], 71), 0),
        "pair_quads": scatter_about(splits[1], (2, NPTS, HALF), (3 * ROWS) ** -0.5, 0.21875, ((1, 512),)),
        "tile_mask": with_ends((jax.random.randint(splits[2], (2, NPTS // TILE, HALF // TILE), 0, 4) < 3).astype(jnp.int32), jax.random.fold_in(splits[2], 1), 0, 1),
        "right_side": draw_right_side(jax.random.fold_in(splits[6], 71), 0),
        "basis": draw_basis(jax.random.fold_in(splits[6], 71), 0),
        "spectrum": jnp.clip(jnp.exp(jax.random.uniform(splits[5], (RANK,), jnp.float32, math.log(0.25), math.log(2.0))), 0.25, 2.0),
    }


LOWER = 0.2
UPPER = 12.0


def reorder(halves, flag):
    flag = flag.reshape(flag.shape + (1,) * (halves.ndim - flag.ndim))
    return jnp.where(flag == 1, halves[:, :, ::-1], halves)


def coupling(quad_blocks, vectors, weight_bit):
    pt_ids = jnp.arange(N_PT, dtype=jnp.int32)
    partner = jnp.bitwise_xor(pt_ids, weight_bit).astype(jnp.int32)
    pair_role = (jnp.bitwise_and(pt_ids, weight_bit) > 0).astype(jnp.int32)
    blocks32 = quad_blocks.astype(jnp.float32)
    partner_vec = reorder(vectors[partner], pair_role)
    local_term = jnp.einsum("psjab,psjbc->psjac", blocks32, partner_vec.astype(jnp.float32))
    transposed = jnp.einsum("psjba,psjbc->psjac", blocks32, vectors.astype(jnp.float32)).astype(jnp.bfloat16)
    returned = reorder(transposed[partner], 1 - pair_role)
    return local_term + returned.astype(jnp.float32)


def apply_operator(kernel_diag, quad_blocks, direction_bf):
    block_count = N_PT * N_SUB
    diag_blocks = kernel_diag.reshape(block_count, ROWS, ROWS).astype(jnp.float32)
    vec_blocks = direction_bf.reshape(block_count, ROWS, RHS).astype(jnp.float32)
    result = jnp.einsum("bkl,blc->bkc", diag_blocks, vec_blocks)
    vectors = direction_bf.reshape(N_PT, N_SUB, 2, HALF, RHS)
    result = result.reshape(N_PT, N_SUB, 2, HALF, RHS)
    result = result + coupling(quad_blocks[0], vectors, 1) + coupling(quad_blocks[1], vectors, N_PT // 2)
    return result.reshape(NPTS, RHS)


def precondition(basis, spectrum, residual):
    coeffs = lax.dot_general(basis, residual, (((0,), (0,)), ((), ())), precision=lax.Precision.HIGHEST)
    scaled = spectrum[:, None] * coeffs
    return 0.5 * residual + (RANK / NPTS) * jnp.dot(basis, scaled, precision=lax.Precision.HIGHEST)


def reference(kernel_diag, pair_quads, tile_mask, right_side, basis, spectrum):
    ones = jnp.repeat(jnp.repeat(tile_mask.astype(jnp.bfloat16), TILE, axis=1), TILE, axis=2)
    quad_blocks = (pair_quads * ones).reshape(2, N_PT, N_SUB, 2, HALF, HALF)
    centre = 0.5 * (UPPER + LOWER)
    radius = 0.5 * (UPPER - LOWER)
    aspect = centre / radius
    ratio_now = 1.0 / aspect
    solution = jnp.zeros_like(right_side)
    residual = right_side
    direction = precondition(basis, spectrum, residual) / centre
    for sweep in range(ITERS):
        direction_bf = direction.astype(jnp.bfloat16)
        solution = solution + direction
        residual = residual - apply_operator(kernel_diag, quad_blocks, direction_bf)
        if sweep + 1 < ITERS:
            precond = precondition(basis, spectrum, residual)
            ratio_next = 1.0 / (2.0 * aspect - ratio_now)
            direction = (ratio_next * ratio_now) * direction + (2.0 * ratio_next / radius) * precond
            ratio_now = ratio_next
    return solution, residual
```

```python
import jax
import jax.numpy as jnp
from jax import lax
from jax.experimental import pallas as pl
from jax.experimental.pallas import tpu as pltpu
from jax.sharding import PartitionSpec as P

ITERS = 2
LOWER = 0.2
UPPER = 12.0
ROWS = 256
HALF = 128
RHS = 64
RANK = 256
N_PT = 64
N_SUB = 8
POINTS = ROWS * N_PT * N_SUB
PLANE = 32
CHIPS = 16
RING = 16
PIECE = (4, 128)
MESH = pl.DeviceIdType.MESH
F32 = jnp.float32
BF16 = jnp.bfloat16


def split(value):
    high = value.astype(BF16)
    return high, (value - high.astype(F32)).astype(BF16)


def dot_nn(left, right):
    return lax.dot_general(left, right, (((1,), (0,)), ((), ())), preferred_element_type=F32)


def dot_nt(left, right):
    return lax.dot_general(left, right, (((1,), (1,)), ((), ())), preferred_element_type=F32)


def send(src, dst, send_sem, recv_sem, device):
    return pltpu.make_async_remote_copy(
        src_ref=src,
        dst_ref=dst,
        send_sem=send_sem,
        recv_sem=recv_sem,
        device_id=device,
        device_id_type=MESH,
    )


def body(
    mask_ref,
    diag_hbm,
    quads_hbm,
    right_hbm,
    basis_hbm,
    spectrum_ref,
    solution_ref,
    residual_ref,
    diag,
    quads,
    right,
    basis,
    basis_hi,
    basis_lo,
    own_quads,
    partner_quads,
    field,
    partner_field,
    coeffs,
    part,
    plane_in,
    plane_sum,
    ring_in,
    ring_sum,
    gathered,
    load_sems,
    quad_send,
    quad_recv,
    field_send,
    field_recv,
    sum_send,
    sum_recv,
):
    pt = lax.axis_index("pt")
    sub = lax.axis_index("sub")
    spot = lax.rem(pt, CHIPS)
    core = lax.rem(sub, 2)
    z_hi = lax.div(pt, CHIPS)
    z_lo = lax.div(sub, 2)
    place = spot * 2 + core
    level = z_hi * 4 + z_lo

    def plane_peer(index):
        return (z_hi * CHIPS + lax.div(index, 2), z_lo * 2 + lax.rem(index, 2))

    def ring_peer(index):
        return (lax.div(index, 4) * CHIPS + spot, lax.rem(index, 4) * 2 + core)

    near_role = lax.rem(pt, 2)
    far_role = lax.div(pt, N_PT // 2)
    partners = (
        (pt + 1 - 2 * near_role, sub),
        (lax.rem(pt + N_PT // 2, N_PT), sub),
    )
    roles = (near_role, far_role)

    loads = [
        pltpu.make_async_copy(src, dst, load_sems.at[i])
        for i, (src, dst) in enumerate(
            ((right_hbm, right), (basis_hbm, basis), (quads_hbm, quads), (diag_hbm, diag))
        )
    ]
    for load in loads:
        load.start()

    barrier = pltpu.get_barrier_semaphore()

    def greet_ring(k, carry):
        pl.semaphore_signal(
            barrier, inc=1, device_id=ring_peer(lax.rem(level + k, RING)), device_id_type=MESH
        )
        return carry

    def greet_plane(k, carry):
        pl.semaphore_signal(
            barrier, inc=1, device_id=plane_peer(lax.rem(place + k, PLANE)), device_id_type=MESH
        )
        return carry

    lax.fori_loop(1, RING, greet_ring, 0)
    lax.fori_loop(1, PLANE, greet_plane, 0)

    def put_part(turn, value):
        coeffs[...] = value
        for i in range(PLANE):
            row, lane = 4 * (i % 16), 128 * (i // 16)
            part[turn, i] = coeffs[row : row + 4, lane : lane + 128]

    def coeff_part(residual):
        high, low = split(residual)
        both = dot_nn(jnp.concatenate([high, low], axis=0), basis_hi[...])
        return both[:RHS] + both[RHS:] + dot_nn(high, basis_lo[...])

    def spread(turn):
        me = part.at[turn]

        def scatter(k, carry):
            peer = lax.rem(place + k, PLANE)
            send(
                me.at[peer],
                plane_in.at[turn, place],
                sum_send.at[turn, 0],
                sum_recv.at[turn, 0],
                plane_peer(peer),
            ).start()
            return carry

        lax.fori_loop(1, PLANE, scatter, 0)
        plane_in[turn, place] = part[turn, place]

    def all_of(ref, count, turn, stage, device):
        span = ref.at[turn, pl.ds(0, count)]
        return send(span, span, sum_send.at[turn, stage], sum_recv.at[turn, stage], device)

    def finish_sum(turn):
        all_of(plane_in, PLANE - 1, turn, 0, partners[0]).wait_recv()
        plane_sum[turn] = jnp.sum(plane_in[turn], axis=0)

        def along(k, carry):
            send(
                plane_sum.at[turn],
                ring_in.at[turn, level],
                sum_send.at[turn, 1],
                sum_recv.at[turn, 1],
                ring_peer(lax.rem(level + k, RING)),
            ).start()
            return carry

        lax.fori_loop(RING // 2, RING, along, 0)
        lax.fori_loop(1, RING // 2, along, 0)
        ring_in[turn, level] = plane_sum[turn]
        all_of(ring_in, RING - 1, turn, 1, partners[0]).wait_recv()
        ring_sum[turn] = jnp.sum(ring_in[turn], axis=0)

        def gather(k, carry):
            send(
                ring_sum.at[turn],
                gathered.at[turn, place],
                sum_send.at[turn, 2],
                sum_recv.at[turn, 2],
                plane_peer(lax.rem(place + k, PLANE)),
            ).start()
            return carry

        lax.fori_loop(1, PLANE, gather, 0)
        gathered[turn, place] = ring_sum[turn]
        all_of(gathered, PLANE - 1, turn, 2, partners[0]).wait_recv()
        for i in range(PLANE):
            row, lane = 4 * (i % 16), 128 * (i // 16)
            coeffs[row : row + 4, lane : lane + 128] = gathered[turn, i]
        return coeffs[...]

    def precondition(residual, summed):
        high, low = split(spectrum_ref[...] * summed)
        both = dot_nt(jnp.concatenate([high, low], axis=0), basis_hi[...])
        term = both[:RHS] + both[RHS:] + dot_nt(high, basis_lo[...])
        return 0.5 * residual + (ROWS / POINTS) * term

    def field_copy(turn, m):
        return send(
            field.at[turn],
            partner_field.at[turn, m],
            field_send.at[turn, m],
            field_recv.at[turn, m],
            partners[m],
        )

    def quad_copy(m):
        return send(
            own_quads.at[m], partner_quads.at[m], quad_send.at[m], quad_recv.at[m], partners[m]
        )

    loads[0].wait()
    residual = right[...].T
    loads[1].wait()
    high, low = split(basis[...])
    basis_hi[...] = high
    basis_lo[...] = low
    put_part(0, coeff_part(residual))
    loads[2].wait()
    for m in range(2):
        for j in range(2):
            keep = mask_ref[m, j, 0].astype(F32)
            rows = quads[m, j * HALF : (j + 1) * HALF, :].astype(F32)
            own_quads[m, j] = (rows * keep).astype(BF16)
    pl.semaphore_wait(barrier, PLANE + RING - 2)

    spread(0)
    for m in range(2):
        quad_copy(m).start()
    loads[3].wait()

    centre = 0.5 * (UPPER + LOWER)
    radius = 0.5 * (UPPER - LOWER)
    aspect = centre / radius
    ratio_now = 1.0 / aspect
    direction = precondition(residual, finish_sum(0)) / centre
    solution = jnp.zeros_like(direction)
    for sweep in range(ITERS):
        direction_bf = direction.astype(BF16)
        field[sweep, 0] = direction_bf[:, :HALF]
        field[sweep, 1] = direction_bf[:, HALF:]
        for m in (1, 0):
            field_copy(sweep, m).start()
        solution = solution + direction
        result = dot_nt(direction_bf, diag[...])
        for m in range(2):
            if sweep == 0:
                quad_copy(m).wait_recv()
            field_copy(sweep, m).wait_recv()
            halves = []
            for j in range(2):
                same = j + roles[m] - 2 * j * roles[m]
                other = 1 - same
                halves.append(
                    dot_nt(partner_field[sweep, m, same], own_quads[m, j])
                    + dot_nn(partner_field[sweep, m, other], partner_quads[m, other])
                )
            result = result + jnp.concatenate(halves, axis=1)
        residual = residual - result
        if sweep + 1 < ITERS:
            put_part(sweep + 1, coeff_part(residual))
            spread(sweep + 1)
            summed = finish_sum(sweep + 1)
            precond = precondition(residual, summed)
            ratio_next = 1.0 / (2.0 * aspect - ratio_now)
            direction = ratio_next * ratio_now * direction + 2.0 * ratio_next / radius * precond
            ratio_now = ratio_next
    solution_ref[...] = solution.T
    residual_ref[...] = residual.T

    for m in range(2):
        quad_copy(m).wait_send()
    for turn in range(ITERS):
        for m in range(2):
            field_copy(turn, m).wait_send()
        all_of(plane_in, PLANE - 1, turn, 0, partners[0]).wait_send()
        all_of(ring_in, RING - 1, turn, 1, partners[0]).wait_send()
        all_of(gathered, PLANE - 1, turn, 2, partners[0]).wait_send()


def on_device(kernel_diag, pair_quads, tile_mask, right_side, basis, spectrum):
    any_spec = pl.BlockSpec(memory_space=pl.ANY)
    vmem_spec = pl.BlockSpec(memory_space=pltpu.VMEM)
    smem_spec = pl.BlockSpec(memory_space=pltpu.SMEM)
    out = jax.ShapeDtypeStruct((ROWS, RHS), F32)
    dma = pltpu.SemaphoreType.DMA
    return pl.pallas_call(
        body,
        name="chebyshev",
        out_shape=(out, out),
        in_specs=[smem_spec, any_spec, any_spec, any_spec, any_spec, vmem_spec],
        out_specs=(vmem_spec, vmem_spec),
        scratch_shapes=[
            pltpu.VMEM((ROWS, ROWS), BF16),
            pltpu.VMEM((2, ROWS, HALF), BF16),
            pltpu.VMEM((ROWS, RHS), F32),
            pltpu.VMEM((ROWS, RANK), F32),
            pltpu.VMEM((ROWS, RANK), BF16),
            pltpu.VMEM((ROWS, RANK), BF16),
            pltpu.VMEM((2, 2, HALF, HALF), BF16),
            pltpu.VMEM((2, 2, HALF, HALF), BF16),
            pltpu.VMEM((ITERS, 2, RHS, HALF), BF16),
            pltpu.VMEM((ITERS, 2, 2, RHS, HALF), BF16),
            pltpu.VMEM((RHS, RANK), F32),
            pltpu.VMEM((ITERS, PLANE, *PIECE), F32),
            pltpu.VMEM((ITERS, PLANE, *PIECE), F32),
            pltpu.VMEM((ITERS, *PIECE), F32),
            pltpu.VMEM((ITERS, RING, *PIECE), F32),
            pltpu.VMEM((ITERS, *PIECE), F32),
            pltpu.VMEM((ITERS, PLANE, *PIECE), F32),
            dma((4,)),
            dma((2,)),
            dma((2,)),
            dma((ITERS, 2)),
            dma((ITERS, 2)),
            dma((ITERS, 3)),
            dma((ITERS, 3)),
        ],
        compiler_params=pltpu.CompilerParams(collective_id=0, has_side_effects=True),
    )(tile_mask, kernel_diag, pair_quads, right_side, basis, spectrum.reshape(1, RANK))


def solution(mesh):
    placed = (
        P(("pt", "sub"), None),
        P(None, ("pt", "sub"), None),
        P(None, ("pt", "sub"), None),
        P(("pt", "sub"), None),
        P(("pt", "sub"), None),
        P(),
    )
    return jax.shard_map(
        on_device,
        mesh=mesh,
        in_specs=placed,
        out_specs=(P(("pt", "sub"), None), P(("pt", "sub"), None)),
        check_vma=False,
    )
```

```python
import jax
import jax.numpy as jnp
from jax import lax
from jax.experimental import pallas as pl
from jax.experimental.pallas import tpu as pltpu
from jax.sharding import PartitionSpec as P

ITERS = 2
LOWER = 0.2
UPPER = 12.0
ROWS = 256
HALF = 128
RHS = 64
RANK = 256
N_PT = 64
N_SUB = 8
POINTS = ROWS * N_PT * N_SUB
PLANE = 32
CHIPS = 16
RING = 16
PIECE = (4, 128)
MESH = pl.DeviceIdType.MESH
F32 = jnp.float32
BF16 = jnp.bfloat16


def split(value):
    high = value.astype(BF16)
    return high, (value - high.astype(F32)).astype(BF16)


def dot_nn(left, right):
    return lax.dot_general(left, right, (((1,), (0,)), ((), ())), preferred_element_type=F32)


def dot_nt(left, right):
    return lax.dot_general(left, right, (((1,), (1,)), ((), ())), preferred_element_type=F32)


def send(src, dst, send_sem, recv_sem, device):
    return pltpu.make_async_remote_copy(
        src_ref=src,
        dst_ref=dst,
        send_sem=send_sem,
        recv_sem=recv_sem,
        device_id=device,
        device_id_type=MESH,
    )


def body(
    mask_ref,
    diag_hbm,
    quads_hbm,
    right_hbm,
    basis_hbm,
    spectrum_ref,
    solution_ref,
    residual_ref,
    diag,
    quads,
    right,
    basis,
    basis_hi,
    basis_lo,
    own_quads,
    partner_quads,
    field,
    partner_field,
    coeffs,
    part,
    plane_in,
    plane_sum,
    ring_in,
    ring_sum,
    gathered,
    load_sems,
    quad_send,
    quad_recv,
    field_send,
    field_recv,
    sum_send,
    sum_recv,
):
    pt = lax.axis_index("pt")
    sub = lax.axis_index("sub")
    spot = lax.rem(pt, CHIPS)
    core = lax.rem(sub, 2)
    z_hi = lax.div(pt, CHIPS)
    z_lo = lax.div(sub, 2)
    place = spot * 2 + core
    level = z_hi * 4 + z_lo

    def plane_peer(index):
        return (z_hi * CHIPS + lax.div(index, 2), z_lo * 2 + lax.rem(index, 2))

    def ring_peer(index):
        return (lax.div(index, 4) * CHIPS + spot, lax.rem(index, 4) * 2 + core)

    near_role = lax.rem(pt, 2)
    far_role = lax.div(pt, N_PT // 2)
    partners = (
        (pt + 1 - 2 * near_role, sub),
        (lax.rem(pt + N_PT // 2, N_PT), sub),
    )
    roles = (near_role, far_role)

    loads = [
        pltpu.make_async_copy(src, dst, load_sems.at[i])
        for i, (src, dst) in enumerate(
            ((right_hbm, right), (basis_hbm, basis), (quads_hbm, quads), (diag_hbm, diag))
        )
    ]
    for load in loads:
        load.start()

    barrier = pltpu.get_barrier_semaphore()

    def greet_ring(k, carry):
        pl.semaphore_signal(
            barrier, inc=1, device_id=ring_peer(lax.rem(level + k, RING)), device_id_type=MESH
        )
        return carry

    def greet_plane(k, carry):
        pl.semaphore_signal(
            barrier, inc=1, device_id=plane_peer(lax.rem(place + k, PLANE)), device_id_type=MESH
        )
        return carry

    lax.fori_loop(1, RING, greet_ring, 0)
    lax.fori_loop(1, PLANE, greet_plane, 0)

    def put_part(turn, value):
        coeffs[...] = value
        for i in range(PLANE):
            row, lane = 4 * (i % 16), 128 * (i // 16)
            part[turn, i] = coeffs[row : row + 4, lane : lane + 128]

    def coeff_part(residual):
        high, low = split(residual)
        both = dot_nn(jnp.concatenate([high, low], axis=0), basis_hi[...])
        return both[:RHS] + both[RHS:] + dot_nn(high, basis_lo[...])

    def spread(turn):
        me = part.at[turn]

        def scatter(k, carry):
            peer = lax.rem(place + k, PLANE)
            send(
                me.at[peer],
                plane_in.at[turn, place],
                sum_send.at[turn, 0],
                sum_recv.at[turn, 0],
                plane_peer(peer),
            ).start()
            return carry

        lax.fori_loop(1, PLANE, scatter, 0)
        plane_in[turn, place] = part[turn, place]

    def all_of(ref, count, turn, stage, device):
        span = ref.at[turn, pl.ds(0, count)]
        return send(span, span, sum_send.at[turn, stage], sum_recv.at[turn, stage], device)

    def finish_sum(turn):
        all_of(plane_in, PLANE - 1, turn, 0, partners[0]).wait_recv()
        plane_sum[turn] = jnp.sum(plane_in[turn], axis=0)

        def along(k, carry):
            send(
                plane_sum.at[turn],
                ring_in.at[turn, level],
                sum_send.at[turn, 1],
                sum_recv.at[turn, 1],
                ring_peer(lax.rem(level + k, RING)),
            ).start()
            return carry

        lax.fori_loop(RING // 2, RING, along, 0)
        lax.fori_loop(1, RING // 2, along, 0)
        ring_in[turn, level] = plane_sum[turn]
        all_of(ring_in, RING - 1, turn, 1, partners[0]).wait_recv()
        ring_sum[turn] = jnp.sum(ring_in[turn], axis=0)

        def gather(k, carry):
            send(
                ring_sum.at[turn],
                gathered.at[turn, place],
                sum_send.at[turn, 2],
                sum_recv.at[turn, 2],
                plane_peer(lax.rem(place + k, PLANE)),
            ).start()
            return carry

        lax.fori_loop(1, PLANE, gather, 0)
        gathered[turn, place] = ring_sum[turn]
        all_of(gathered, PLANE - 1, turn, 2, partners[0]).wait_recv()
        for i in range(PLANE):
            row, lane = 4 * (i % 16), 128 * (i // 16)
            coeffs[row : row + 4, lane : lane + 128] = gathered[turn, i]
        return coeffs[...]

    def precondition(residual, summed):
        high, low = split(spectrum_ref[...] * summed)
        both = dot_nt(jnp.concatenate([high, low], axis=0), basis_hi[...])
        term = both[:RHS] + both[RHS:] + dot_nt(high, basis_lo[...])
        return 0.5 * residual + (ROWS / POINTS) * term

    def field_copy(turn, m):
        return send(
            field.at[turn],
            partner_field.at[turn, m],
            field_send.at[turn, m],
            field_recv.at[turn, m],
            partners[m],
        )

    def quad_copy(m):
        return send(
            own_quads.at[m], partner_quads.at[m], quad_send.at[m], quad_recv.at[m], partners[m]
        )

    loads[0].wait()
    residual = right[...]
    loads[1].wait()
    high, low = split(basis[...])
    basis_hi[...] = high
    basis_lo[...] = low
    put_part(0, coeff_part(residual))
    loads[2].wait()
    for m in range(2):
        for j in range(2):
            keep = mask_ref[m, 0, j].astype(F32)
            rows = quads[m, j * HALF : (j + 1) * HALF, :].astype(F32)
            own_quads[m, j] = (rows * keep).astype(BF16)
    pl.semaphore_wait(barrier, PLANE + RING - 2)

    spread(0)
    for m in range(2):
        quad_copy(m).start()
    loads[3].wait()

    centre = 0.5 * (UPPER + LOWER)
    radius = 0.5 * (UPPER - LOWER)
    aspect = centre / radius
    ratio_now = 1.0 / aspect
    direction = precondition(residual, finish_sum(0)) / centre
    solution = jnp.zeros_like(direction)
    for sweep in range(ITERS):
        direction_bf = direction.astype(BF16)
        field[sweep, 0] = direction_bf[:, :HALF]
        field[sweep, 1] = direction_bf[:, HALF:]
        for m in (1, 0):
            field_copy(sweep, m).start()
        solution = solution + direction
        result = dot_nt(direction_bf, diag[...])
        for m in range(2):
            if sweep == 0:
                quad_copy(m).wait_recv()
            field_copy(sweep, m).wait_recv()
            halves = []
            for j in range(2):
                same = j + roles[m] - 2 * j * roles[m]
                other = 1 - same
                halves.append(
                    dot_nt(partner_field[sweep, m, same], own_quads[m, j])
                    + dot_nn(partner_field[sweep, m, other], partner_quads[m, other])
                )
            result = result + jnp.concatenate(halves, axis=1)
        residual = residual - result
        if sweep + 1 < ITERS:
            put_part(sweep + 1, coeff_part(residual))
            spread(sweep + 1)
            summed = finish_sum(sweep + 1)
            precond = precondition(residual, summed)
            ratio_next = 1.0 / (2.0 * aspect - ratio_now)
            direction = ratio_next * ratio_now * direction + 2.0 * ratio_next / radius * precond
            ratio_now = ratio_next
    solution_ref[...] = solution
    residual_ref[...] = residual

    for m in range(2):
        quad_copy(m).wait_send()
    for turn in range(ITERS):
        for m in range(2):
            field_copy(turn, m).wait_send()
        all_of(plane_in, PLANE - 1, turn, 0, partners[0]).wait_send()
        all_of(ring_in, RING - 1, turn, 1, partners[0]).wait_send()
        all_of(gathered, PLANE - 1, turn, 2, partners[0]).wait_send()


def on_device(kernel_diag, pair_quads, tile_mask, right_side, basis, spectrum):
    any_spec = pl.BlockSpec(memory_space=pl.ANY)
    vmem_spec = pl.BlockSpec(memory_space=pltpu.VMEM)
    smem_spec = pl.BlockSpec(memory_space=pltpu.SMEM)
    out = jax.ShapeDtypeStruct((RHS, ROWS), F32)
    dma = pltpu.SemaphoreType.DMA
    solved, left = pl.pallas_call(
        body,
        name="chebyshev",
        out_shape=(out, out),
        in_specs=[smem_spec, any_spec, any_spec, any_spec, any_spec, vmem_spec],
        out_specs=(vmem_spec, vmem_spec),
        scratch_shapes=[
            pltpu.VMEM((ROWS, ROWS), BF16),
            pltpu.VMEM((2, ROWS, HALF), BF16),
            pltpu.VMEM((RHS, ROWS), F32),
            pltpu.VMEM((ROWS, RANK), F32),
            pltpu.VMEM((ROWS, RANK), BF16),
            pltpu.VMEM((ROWS, RANK), BF16),
            pltpu.VMEM((2, 2, HALF, HALF), BF16),
            pltpu.VMEM((2, 2, HALF, HALF), BF16),
            pltpu.VMEM((ITERS, 2, RHS, HALF), BF16),
            pltpu.VMEM((ITERS, 2, 2, RHS, HALF), BF16),
            pltpu.VMEM((RHS, RANK), F32),
            pltpu.VMEM((ITERS, PLANE, *PIECE), F32),
            pltpu.VMEM((ITERS, PLANE, *PIECE), F32),
            pltpu.VMEM((ITERS, *PIECE), F32),
            pltpu.VMEM((ITERS, RING, *PIECE), F32),
            pltpu.VMEM((ITERS, *PIECE), F32),
            pltpu.VMEM((ITERS, PLANE, *PIECE), F32),
            dma((4,)),
            dma((2,)),
            dma((2,)),
            dma((ITERS, 2)),
            dma((ITERS, 2)),
            dma((ITERS, 3)),
            dma((ITERS, 3)),
        ],
        compiler_params=pltpu.CompilerParams(collective_id=0, has_side_effects=True),
    )(
        jnp.swapaxes(tile_mask, 1, 2),
        kernel_diag,
        pair_quads,
        right_side.T,
        basis,
        spectrum.reshape(1, RANK),
    )
    return solved.T, left.T


def solution(mesh):
    placed = (
        P(("pt", "sub"), None),
        P(None, ("pt", "sub"), None),
        P(None, ("pt", "sub"), None),
        P(("pt", "sub"), None),
        P(("pt", "sub"), None),
        P(),
    )
    return jax.shard_map(
        on_device,
        mesh=mesh,
        in_specs=placed,
        out_specs=(P(("pt", "sub"), None), P(("pt", "sub"), None)),
        check_vma=False,
    )
```

```python
import jax
import jax.numpy as jnp
from jax import lax
from jax.experimental import pallas as pl
from jax.experimental.pallas import tpu as pltpu
from jax.sharding import PartitionSpec as P

ITERS = 2
LOWER = 0.2
UPPER = 12.0
ROWS = 256
HALF = 128
RHS = 64
RANK = 256
N_PT = 64
N_SUB = 8
POINTS = ROWS * N_PT * N_SUB
PLANE = 32
CHIPS = 16
RING = 16
PIECE = (4, 128)
CHUNK = 64
MESH = pl.DeviceIdType.MESH
F32 = jnp.float32
BF16 = jnp.bfloat16


def split(value):
    high = value.astype(BF16)
    return high, (value - high.astype(F32)).astype(BF16)


def dot_nn(left, right):
    return lax.dot_general(left, right, (((1,), (0,)), ((), ())), preferred_element_type=F32)


def dot_nt(left, right):
    return lax.dot_general(left, right, (((1,), (1,)), ((), ())), preferred_element_type=F32)


def send(src, dst, send_sem, recv_sem, device):
    return pltpu.make_async_remote_copy(
        src_ref=src,
        dst_ref=dst,
        send_sem=send_sem,
        recv_sem=recv_sem,
        device_id=device,
        device_id_type=MESH,
    )


def body(
    mask_ref,
    diag_hbm,
    quads_hbm,
    right_hbm,
    basis_hbm,
    spectrum_ref,
    solution_ref,
    residual_ref,
    diag,
    quads,
    right,
    basis,
    basis_hi,
    basis_lo,
    own_quads,
    partner_quads,
    field,
    partner_field,
    partner_basis,
    known,
    partner_known,
    coeffs,
    part,
    plane_in,
    plane_sum,
    ring_in,
    ring_sum,
    gathered,
    load_sems,
    quad_send,
    quad_recv,
    field_send,
    field_recv,
    basis_send,
    basis_recv,
    known_send,
    known_recv,
    sum_send,
    sum_recv,
):
    pt = lax.axis_index("pt")
    sub = lax.axis_index("sub")
    spot = lax.rem(pt, CHIPS)
    core = lax.rem(sub, 2)
    z_hi = lax.div(pt, CHIPS)
    z_lo = lax.div(sub, 2)
    place = spot * 2 + core
    level = z_hi * 4 + z_lo

    def plane_peer(index):
        return (z_hi * CHIPS + lax.div(index, 2), z_lo * 2 + lax.rem(index, 2))

    def ring_peer(index):
        return (lax.div(index, 4) * CHIPS + spot, lax.rem(index, 4) * 2 + core)

    near_role = lax.rem(pt, 2)
    far_role = lax.div(pt, N_PT // 2)
    partners = (
        (pt + 1 - 2 * near_role, sub),
        (lax.rem(pt + N_PT // 2, N_PT), sub),
    )
    roles = (near_role, far_role)

    loads = [
        pltpu.make_async_copy(src, dst, load_sems.at[i])
        for i, (src, dst) in enumerate(
            ((right_hbm, right), (basis_hbm, basis), (quads_hbm, quads), (diag_hbm, diag))
        )
    ]
    for load in loads:
        load.start()

    barrier = pltpu.get_barrier_semaphore()

    def greet_ring(k, carry):
        pl.semaphore_signal(
            barrier, inc=1, device_id=ring_peer(lax.rem(level + k, RING)), device_id_type=MESH
        )
        return carry

    def greet_plane(k, carry):
        pl.semaphore_signal(
            barrier, inc=1, device_id=plane_peer(lax.rem(place + k, PLANE)), device_id_type=MESH
        )
        return carry

    lax.fori_loop(1, RING, greet_ring, 0)
    lax.fori_loop(1, PLANE, greet_plane, 0)

    def put_part(turn, value):
        coeffs[...] = value
        for i in range(PLANE):
            row, lane = 4 * (i % 16), 128 * (i // 16)
            part[turn, i] = coeffs[row : row + 4, lane : lane + 128]

    def coeff_part(residual):
        high, low = split(residual)
        both = dot_nn(jnp.concatenate([high, low], axis=0), basis_hi[...])
        return both[:RHS] + both[RHS:] + dot_nn(high, basis_lo[...])

    def spread(turn):
        me = part.at[turn]

        def scatter(k, carry):
            peer = lax.rem(place + k, PLANE)
            send(
                me.at[peer],
                plane_in.at[turn, place],
                sum_send.at[turn, 0],
                sum_recv.at[turn, 0],
                plane_peer(peer),
            ).start()
            return carry

        lax.fori_loop(1, PLANE, scatter, 0)
        plane_in[turn, place] = part[turn, place]

    def all_of(ref, count, turn, stage, device):
        span = ref.at[turn, pl.ds(0, count)]
        return send(span, span, sum_send.at[turn, stage], sum_recv.at[turn, stage], device)

    def finish_sum(turn):
        all_of(plane_in, PLANE - 1, turn, 0, partners[0]).wait_recv()
        plane_sum[turn] = jnp.sum(plane_in[turn], axis=0)

        def along(k, carry):
            send(
                plane_sum.at[turn],
                ring_in.at[turn, level],
                sum_send.at[turn, 1],
                sum_recv.at[turn, 1],
                ring_peer(lax.rem(level + k, RING)),
            ).start()
            return carry

        lax.fori_loop(RING // 2, RING, along, 0)
        lax.fori_loop(1, RING // 2, along, 0)
        ring_in[turn, level] = plane_sum[turn]
        all_of(ring_in, RING - 1, turn, 1, partners[0]).wait_recv()
        ring_sum[turn] = jnp.sum(ring_in[turn], axis=0)

        def gather(k, carry):
            send(
                ring_sum.at[turn],
                gathered.at[turn, place],
                sum_send.at[turn, 2],
                sum_recv.at[turn, 2],
                plane_peer(lax.rem(place + k, PLANE)),
            ).start()
            return carry

        lax.fori_loop(1, PLANE, gather, 0)
        gathered[turn, place] = ring_sum[turn]
        all_of(gathered, PLANE - 1, turn, 2, partners[0]).wait_recv()
        for i in range(PLANE):
            row, lane = 4 * (i % 16), 128 * (i // 16)
            coeffs[row : row + 4, lane : lane + 128] = gathered[turn, i]
        return coeffs[...]

    def scaled(summed):
        return split(ROWS / POINTS * spectrum_ref[...] * summed)

    def low_rank(pair, basis_rows):
        both = dot_nt(jnp.concatenate(pair, axis=0), basis_rows)
        return both[:RHS] + both[RHS:]

    def field_copy(m):
        return send(
            field,
            partner_field.at[m],
            field_send.at[m],
            field_recv.at[m],
            partners[m],
        )

    def quad_copy(m):
        return send(
            own_quads.at[m], partner_quads.at[m], quad_send.at[m], quad_recv.at[m], partners[m]
        )

    def basis_copy(m, chunk):
        rows = pl.ds(chunk * CHUNK, CHUNK)
        return send(
            basis_hi.at[rows],
            partner_basis.at[m, rows],
            basis_send.at[m, chunk],
            basis_recv.at[m, chunk],
            partners[m],
        )

    def known_copy(m):
        return send(known, partner_known.at[m], known_send.at[m], known_recv.at[m], partners[m])

    def put_halves(ref, value):
        ref[0] = value[:, :HALF]
        ref[1] = value[:, HALF:]

    def coupled(m):
        halves = []
        for j in range(2):
            same = j + roles[m] - 2 * j * roles[m]
            other = 1 - same
            halves.append(
                dot_nt(partner_field[m, same], own_quads[m, j])
                + dot_nn(partner_field[m, other], partner_quads[m, other])
            )
        return jnp.concatenate(halves, axis=1)

    loads[0].wait()
    residual = right[...]
    loads[1].wait()
    high, low = split(basis[...])
    basis_hi[...] = high
    basis_lo[...] = low
    put_part(0, coeff_part(residual))
    loads[2].wait()
    for m in range(2):
        for j in range(2):
            keep = mask_ref[m, 0, j].astype(F32)
            rows = quads[m, j * HALF : (j + 1) * HALF, :].astype(F32)
            own_quads[m, j] = (rows * keep).astype(BF16)
    pl.semaphore_wait(barrier, PLANE + RING - 2)

    spread(0)
    for m in range(2):
        quad_copy(m).start()
    loads[3].wait()

    centre = 0.5 * (UPPER + LOWER)
    radius = 0.5 * (UPPER - LOWER)
    aspect = centre / radius
    ratio_now = 1.0 / aspect
    ratio_next = 1.0 / (2.0 * aspect - ratio_now)
    gain = 2.0 * ratio_next / radius
    pair = scaled(finish_sum(0))
    term = low_rank(pair, basis_hi[...]) + dot_nt(pair[0], basis_lo[...])
    solution = (0.5 * residual + term) / centre

    direction_bf = solution.astype(BF16)
    put_halves(field, direction_bf)
    for m in (1, 0):
        field_copy(m).start()
    for chunk in range(ROWS // CHUNK):
        for m in (1, 0):
            basis_copy(m, chunk).start()
    residual = residual - dot_nt(direction_bf, diag[...])
    for m in range(2):
        quad_copy(m).wait_recv()
        field_copy(m).wait_recv()
        residual = residual - coupled(m)

    put_part(1, coeff_part(residual))
    spread(1)
    direction = ratio_next * ratio_now * solution + 0.5 * gain * residual
    known[...] = direction.astype(BF16)
    for m in (1, 0):
        known_copy(m).start()
    for m in range(2):
        field_copy(m).wait_send()
    pair = scaled(finish_sum(1))
    term = low_rank(pair, basis_hi[...]) + dot_nt(pair[0], basis_lo[...])
    direction = direction + gain * term
    solution_ref[...] = solution + direction
    residual = residual - dot_nt(direction.astype(BF16), diag[...])
    for m in range(2):
        for chunk in range(ROWS // CHUNK):
            basis_copy(m, chunk).wait_recv()
        known_copy(m).wait_recv()
        theirs = partner_known[m].astype(F32) + gain * low_rank(pair, partner_basis[m])
        put_halves(partner_field.at[m], theirs.astype(BF16))
        residual = residual - coupled(m)
    residual_ref[...] = residual

    for m in range(2):
        quad_copy(m).wait_send()
        known_copy(m).wait_send()
        for chunk in range(ROWS // CHUNK):
            basis_copy(m, chunk).wait_send()
    for turn in range(ITERS):
        all_of(plane_in, PLANE - 1, turn, 0, partners[0]).wait_send()
        all_of(ring_in, RING - 1, turn, 1, partners[0]).wait_send()
        all_of(gathered, PLANE - 1, turn, 2, partners[0]).wait_send()


def on_device(kernel_diag, pair_quads, tile_mask, right_side, basis, spectrum):
    any_spec = pl.BlockSpec(memory_space=pl.ANY)
    vmem_spec = pl.BlockSpec(memory_space=pltpu.VMEM)
    smem_spec = pl.BlockSpec(memory_space=pltpu.SMEM)
    out = jax.ShapeDtypeStruct((RHS, ROWS), F32)
    dma = pltpu.SemaphoreType.DMA
    solved, left = pl.pallas_call(
        body,
        name="chebyshev",
        out_shape=(out, out),
        in_specs=[smem_spec, any_spec, any_spec, any_spec, any_spec, vmem_spec],
        out_specs=(vmem_spec, vmem_spec),
        scratch_shapes=[
            pltpu.VMEM((ROWS, ROWS), BF16),
            pltpu.VMEM((2, ROWS, HALF), BF16),
            pltpu.VMEM((RHS, ROWS), F32),
            pltpu.VMEM((ROWS, RANK), F32),
            pltpu.VMEM((ROWS, RANK), BF16),
            pltpu.VMEM((ROWS, RANK), BF16),
            pltpu.VMEM((2, 2, HALF, HALF), BF16),
            pltpu.VMEM((2, 2, HALF, HALF), BF16),
            pltpu.VMEM((2, RHS, HALF), BF16),
            pltpu.VMEM((2, 2, RHS, HALF), BF16),
            pltpu.VMEM((2, ROWS, RANK), BF16),
            pltpu.VMEM((RHS, ROWS), BF16),
            pltpu.VMEM((2, RHS, ROWS), BF16),
            pltpu.VMEM((RHS, RANK), F32),
            pltpu.VMEM((ITERS, PLANE, *PIECE), F32),
            pltpu.VMEM((ITERS, PLANE, *PIECE), F32),
            pltpu.VMEM((ITERS, *PIECE), F32),
            pltpu.VMEM((ITERS, RING, *PIECE), F32),
            pltpu.VMEM((ITERS, *PIECE), F32),
            pltpu.VMEM((ITERS, PLANE, *PIECE), F32),
            dma((4,)),
            dma((2,)),
            dma((2,)),
            dma((2,)),
            dma((2,)),
            dma((2, ROWS // CHUNK)),
            dma((2, ROWS // CHUNK)),
            dma((2,)),
            dma((2,)),
            dma((ITERS, 3)),
            dma((ITERS, 3)),
        ],
        compiler_params=pltpu.CompilerParams(collective_id=0, has_side_effects=True),
    )(
        jnp.swapaxes(tile_mask, 1, 2),
        kernel_diag,
        pair_quads,
        right_side.T,
        basis,
        spectrum.reshape(1, RANK),
    )
    return solved.T, left.T


def solution(mesh):
    placed = (
        P(("pt", "sub"), None),
        P(None, ("pt", "sub"), None),
        P(None, ("pt", "sub"), None),
        P(("pt", "sub"), None),
        P(("pt", "sub"), None),
        P(),
    )
    return jax.shard_map(
        on_device,
        mesh=mesh,
        in_specs=placed,
        out_specs=(P(("pt", "sub"), None), P(("pt", "sub"), None)),
        check_vma=False,
    )
```

```python
import jax
import jax.numpy as jnp
from jax import lax
from jax.experimental import pallas as pl
from jax.experimental.pallas import tpu as pltpu
from jax.sharding import PartitionSpec as P

ITERS = 2
LOWER = 0.2
UPPER = 12.0
ROWS = 256
HALF = 128
RHS = 64
RANK = 256
N_PT = 64
N_SUB = 8
POINTS = ROWS * N_PT * N_SUB
PLANE = 32
CHIPS = 16
RING = 16
PIECE = (4, 128)
FAR_FIRST = 12
MESH = pl.DeviceIdType.MESH
F32 = jnp.float32
BF16 = jnp.bfloat16
PLANE_TYPE = BF16
RING_TYPE = BF16
GATHER_TYPE = F32
CHUNK = 32
BASIS_AT = (4, 4)


def split(value):
    high = value.astype(BF16)
    return high, (value - high.astype(F32)).astype(BF16)


def dot_nn(left, right):
    return lax.dot_general(left, right, (((1,), (0,)), ((), ())), preferred_element_type=F32)


def dot_nt(left, right):
    return lax.dot_general(left, right, (((1,), (1,)), ((), ())), preferred_element_type=F32)


def send(src, dst, send_sem, recv_sem, device):
    return pltpu.make_async_remote_copy(
        src_ref=src,
        dst_ref=dst,
        send_sem=send_sem,
        recv_sem=recv_sem,
        device_id=device,
        device_id_type=MESH,
    )


def body(
    mask_ref,
    diag_hbm,
    quads_hbm,
    right_hbm,
    basis_hbm,
    spectrum_ref,
    solution_ref,
    residual_ref,
    diag,
    quads,
    right,
    basis,
    basis_hi,
    basis_lo,
    own_quads,
    partner_quads,
    field,
    partner_field,
    partner_basis,
    known,
    partner_known,
    coeffs,
    part,
    plane_in,
    plane_sum,
    ring_in,
    ring_sum,
    gathered,
    load_sems,
    quad_send,
    quad_recv,
    field_send,
    field_recv,
    basis_send,
    basis_recv,
    known_send,
    known_recv,
    sum_send,
    sum_recv,
):
    pt = lax.axis_index("pt")
    sub = lax.axis_index("sub")
    spot = lax.rem(pt, CHIPS)
    core = lax.rem(sub, 2)
    z_hi = lax.div(pt, CHIPS)
    z_lo = lax.div(sub, 2)
    place = spot * 2 + core
    level = z_hi * 4 + z_lo

    def plane_peer(index):
        return (z_hi * CHIPS + lax.div(index, 2), z_lo * 2 + lax.rem(index, 2))

    def ring_peer(index):
        return (lax.div(index, 4) * CHIPS + spot, lax.rem(index, 4) * 2 + core)

    near_role = lax.rem(pt, 2)
    far_role = lax.div(pt, N_PT // 2)
    partners = (
        (pt + 1 - 2 * near_role, sub),
        (lax.rem(pt + N_PT // 2, N_PT), sub),
    )
    roles = (near_role, far_role)

    loads = [
        pltpu.make_async_copy(src, dst, load_sems.at[i])
        for i, (src, dst) in enumerate(
            ((right_hbm, right), (basis_hbm, basis), (quads_hbm, quads), (diag_hbm, diag))
        )
    ]
    for load in loads:
        load.start()

    barrier = pltpu.get_barrier_semaphore()

    def greet_ring(k, carry):
        pl.semaphore_signal(
            barrier, inc=1, device_id=ring_peer(lax.rem(level + k, RING)), device_id_type=MESH
        )
        return carry

    def greet_plane(k, carry):
        pl.semaphore_signal(
            barrier, inc=1, device_id=plane_peer(lax.rem(place + k, PLANE)), device_id_type=MESH
        )
        return carry

    lax.fori_loop(1, RING, greet_ring, 0)
    lax.fori_loop(1, PLANE, greet_plane, 0)

    def put_part(turn, value):
        coeffs[...] = value
        for i in range(PLANE):
            row, lane = 4 * (i % 16), 128 * (i // 16)
            part[turn, i] = coeffs[row : row + 4, lane : lane + 128].astype(PLANE_TYPE)

    def coeff_part(residual):
        high, low = split(residual)
        both = dot_nn(jnp.concatenate([high, low], axis=0), basis_hi[...])
        return both[:RHS] + both[RHS:] + dot_nn(high, basis_lo[...])

    def spread(turn):
        me = part.at[turn]

        def scatter(k, carry):
            peer = lax.rem(place + k, PLANE)
            send(
                me.at[peer],
                plane_in.at[turn, place],
                sum_send.at[turn, 0],
                sum_recv.at[turn, 0],
                plane_peer(peer),
            ).start()
            return carry

        lax.fori_loop(FAR_FIRST, PLANE, scatter, 0)
        lax.fori_loop(1, FAR_FIRST, scatter, 0)
        plane_in[turn, place] = part[turn, place]

    def all_of(ref, count, turn, stage, device):
        span = ref.at[turn, pl.ds(0, count)]
        return send(span, span, sum_send.at[turn, stage], sum_recv.at[turn, stage], device)

    def finish_sum(turn, meanwhile=None):
        all_of(plane_in, PLANE - 1, turn, 0, partners[0]).wait_recv()
        plane_sum[turn] = jnp.sum(plane_in[turn].astype(F32), axis=0).astype(RING_TYPE)

        def along(k, carry):
            send(
                plane_sum.at[turn],
                ring_in.at[turn, level],
                sum_send.at[turn, 1],
                sum_recv.at[turn, 1],
                ring_peer(lax.rem(level + k, RING)),
            ).start()
            return carry

        lax.fori_loop(RING // 2, RING, along, 0)
        lax.fori_loop(1, RING // 2, along, 0)
        ring_in[turn, level] = plane_sum[turn]
        all_of(ring_in, RING - 1, turn, 1, partners[0]).wait_recv()
        ring_sum[turn] = jnp.sum(ring_in[turn].astype(F32), axis=0).astype(GATHER_TYPE)

        def gather(k, carry):
            send(
                ring_sum.at[turn],
                gathered.at[turn, place],
                sum_send.at[turn, 2],
                sum_recv.at[turn, 2],
                plane_peer(lax.rem(place + k, PLANE)),
            ).start()
            return carry

        lax.fori_loop(FAR_FIRST, PLANE, gather, 0)
        lax.fori_loop(1, FAR_FIRST, gather, 0)
        gathered[turn, place] = ring_sum[turn]
        if meanwhile is not None:
            meanwhile()
        all_of(gathered, PLANE - 1, turn, 2, partners[0]).wait_recv()
        for i in range(PLANE):
            row, lane = 4 * (i % 16), 128 * (i // 16)
            coeffs[row : row + 4, lane : lane + 128] = gathered[turn, i].astype(F32)
        return coeffs[...]

    def scaled(summed):
        return split(ROWS / POINTS * spectrum_ref[...] * summed)

    def low_rank(pair, basis_rows):
        both = dot_nt(jnp.concatenate(pair, axis=0), basis_rows)
        return both[:RHS] + both[RHS:]

    def field_copy(m):
        return send(
            field,
            partner_field.at[m],
            field_send.at[m],
            field_recv.at[m],
            partners[m],
        )

    def quad_copy(m):
        return send(
            own_quads.at[m], partner_quads.at[m], quad_send.at[m], quad_recv.at[m], partners[m]
        )

    def basis_copy(m, chunk):
        rows = pl.ds(chunk * CHUNK, CHUNK)
        return send(
            basis_hi.at[rows],
            partner_basis.at[m, rows],
            basis_send.at[m, chunk],
            basis_recv.at[m, chunk],
            partners[m],
        )

    def send_basis(point):
        first = sum(BASIS_AT[:point])
        for chunk in range(first, first + BASIS_AT[point]):
            for m in (1, 0):
                basis_copy(m, chunk).start()

    def known_copy(m):
        return send(known, partner_known.at[m], known_send.at[m], known_recv.at[m], partners[m])

    def put_halves(ref, value):
        ref[0] = value[:, :HALF]
        ref[1] = value[:, HALF:]

    def coupled(m):
        halves = []
        for j in range(2):
            same = j + roles[m] - 2 * j * roles[m]
            other = 1 - same
            halves.append(
                dot_nt(partner_field[m, same], own_quads[m, j])
                + dot_nn(partner_field[m, other], partner_quads[m, other])
            )
        return jnp.concatenate(halves, axis=1)

    loads[0].wait()
    residual = right[...]
    loads[1].wait()
    high, low = split(basis[...])
    basis_hi[...] = high
    basis_lo[...] = low
    put_part(0, coeff_part(residual))
    loads[2].wait()
    for m in range(2):
        for j in range(2):
            keep = mask_ref[m, 0, j].astype(F32)
            rows = quads[m, j * HALF : (j + 1) * HALF, :].astype(F32)
            own_quads[m, j] = (rows * keep).astype(BF16)
    pl.semaphore_wait(barrier, PLANE + RING - 2)

    spread(0)
    for m in (1, 0):
        quad_copy(m).start()
    loads[3].wait()

    centre = 0.5 * (UPPER + LOWER)
    radius = 0.5 * (UPPER - LOWER)
    aspect = centre / radius
    ratio_now = 1.0 / aspect
    ratio_next = 1.0 / (2.0 * aspect - ratio_now)
    gain = 2.0 * ratio_next / radius
    pair = scaled(finish_sum(0, lambda: send_basis(0)))
    term = low_rank(pair, basis_hi[...]) + dot_nt(pair[0], basis_lo[...])
    solution = (0.5 * residual + term) / centre

    direction_bf = solution.astype(BF16)
    put_halves(field, direction_bf)
    for m in (1, 0):
        field_copy(m).start()
    residual = residual - dot_nt(direction_bf, diag[...])
    for m in range(2):
        quad_copy(m).wait_recv()
        field_copy(m).wait_recv()
        residual = residual - coupled(m)

    send_basis(1)
    put_part(1, coeff_part(residual))
    spread(1)
    direction = ratio_next * ratio_now * solution + 0.5 * gain * residual
    known[...] = direction.astype(BF16)
    for m in (1, 0):
        known_copy(m).start()
    for m in range(2):
        field_copy(m).wait_send()
    pair = scaled(finish_sum(1))
    term = low_rank(pair, basis_hi[...]) + dot_nt(pair[0], basis_lo[...])
    direction = direction + gain * term
    solution_ref[...] = solution + direction
    residual = residual - dot_nt(direction.astype(BF16), diag[...])
    for m in range(2):
        for chunk in range(ROWS // CHUNK):
            basis_copy(m, chunk).wait_recv()
        known_copy(m).wait_recv()
        theirs = partner_known[m].astype(F32) + gain * low_rank(pair, partner_basis[m])
        put_halves(partner_field.at[m], theirs.astype(BF16))
        residual = residual - coupled(m)
    residual_ref[...] = residual

    for m in range(2):
        quad_copy(m).wait_send()
        known_copy(m).wait_send()
        for chunk in range(ROWS // CHUNK):
            basis_copy(m, chunk).wait_send()
    for turn in range(ITERS):
        all_of(plane_in, PLANE - 1, turn, 0, partners[0]).wait_send()
        all_of(ring_in, RING - 1, turn, 1, partners[0]).wait_send()
        all_of(gathered, PLANE - 1, turn, 2, partners[0]).wait_send()


def on_device(kernel_diag, pair_quads, tile_mask, right_side, basis, spectrum):
    any_spec = pl.BlockSpec(memory_space=pl.ANY)
    vmem_spec = pl.BlockSpec(memory_space=pltpu.VMEM)
    smem_spec = pl.BlockSpec(memory_space=pltpu.SMEM)
    out = jax.ShapeDtypeStruct((RHS, ROWS), F32)
    dma = pltpu.SemaphoreType.DMA
    solved, left = pl.pallas_call(
        body,
        name="chebyshev",
        out_shape=(out, out),
        in_specs=[smem_spec, any_spec, any_spec, any_spec, any_spec, vmem_spec],
        out_specs=(vmem_spec, vmem_spec),
        scratch_shapes=[
            pltpu.VMEM((ROWS, ROWS), BF16),
            pltpu.VMEM((2, ROWS, HALF), BF16),
            pltpu.VMEM((RHS, ROWS), F32),
            pltpu.VMEM((ROWS, RANK), F32),
            pltpu.VMEM((ROWS, RANK), BF16),
            pltpu.VMEM((ROWS, RANK), BF16),
            pltpu.VMEM((2, 2, HALF, HALF), BF16),
            pltpu.VMEM((2, 2, HALF, HALF), BF16),
            pltpu.VMEM((2, RHS, HALF), BF16),
            pltpu.VMEM((2, 2, RHS, HALF), BF16),
            pltpu.VMEM((2, ROWS, RANK), BF16),
            pltpu.VMEM((RHS, ROWS), BF16),
            pltpu.VMEM((2, RHS, ROWS), BF16),
            pltpu.VMEM((RHS, RANK), F32),
            pltpu.VMEM((ITERS, PLANE, *PIECE), PLANE_TYPE),
            pltpu.VMEM((ITERS, PLANE, *PIECE), PLANE_TYPE),
            pltpu.VMEM((ITERS, *PIECE), RING_TYPE),
            pltpu.VMEM((ITERS, RING, *PIECE), RING_TYPE),
            pltpu.VMEM((ITERS, *PIECE), GATHER_TYPE),
            pltpu.VMEM((ITERS, PLANE, *PIECE), GATHER_TYPE),
            dma((4,)),
            dma((2,)),
            dma((2,)),
            dma((2,)),
            dma((2,)),
            dma((2, ROWS // CHUNK)),
            dma((2, ROWS // CHUNK)),
            dma((2,)),
            dma((2,)),
            dma((ITERS, 3)),
            dma((ITERS, 3)),
        ],
        compiler_params=pltpu.CompilerParams(collective_id=0, has_side_effects=True),
    )(
        jnp.swapaxes(tile_mask, 1, 2),
        kernel_diag,
        pair_quads,
        right_side.T,
        basis,
        spectrum.reshape(1, RANK),
    )
    return solved.T, left.T


def solution(mesh):
    placed = (
        P(("pt", "sub"), None),
        P(None, ("pt", "sub"), None),
        P(None, ("pt", "sub"), None),
        P(("pt", "sub"), None),
        P(("pt", "sub"), None),
        P(),
    )
    return jax.shard_map(
        on_device,
        mesh=mesh,
        in_specs=placed,
        out_specs=(P(("pt", "sub"), None), P(("pt", "sub"), None)),
        check_vma=False,
    )
```

```python
import jax
import jax.numpy as jnp
from jax import lax
from jax.experimental import pallas as pl
from jax.experimental.pallas import tpu as pltpu
from jax.sharding import PartitionSpec as P

ITERS = 2
LOWER = 0.2
UPPER = 12.0
ROWS = 256
HALF = 128
RHS = 64
RANK = 256
N_PT = 64
N_SUB = 8
POINTS = ROWS * N_PT * N_SUB
PLANE = 32
CHIPS = 16
RING = 16
PIECE = (4, 128)
FAR_FIRST = 12
MESH = pl.DeviceIdType.MESH
F32 = jnp.float32
BF16 = jnp.bfloat16
PLANE_TYPE = BF16
RING_TYPE = BF16
GATHER_TYPE = F32
CHUNK = 32
BASIS_AT = (4, 4)


def split(value):
    high = value.astype(BF16)
    return high, (value - high.astype(F32)).astype(BF16)


def dot_nn(left, right):
    return lax.dot_general(left, right, (((1,), (0,)), ((), ())), preferred_element_type=F32)


def dot_nt(left, right):
    return lax.dot_general(left, right, (((1,), (1,)), ((), ())), preferred_element_type=F32)


def send(src, dst, send_sem, recv_sem, device):
    return pltpu.make_async_remote_copy(
        src_ref=src,
        dst_ref=dst,
        send_sem=send_sem,
        recv_sem=recv_sem,
        device_id=device,
        device_id_type=MESH,
    )


def body(
    mask_ref,
    diag_hbm,
    quads_hbm,
    right_hbm,
    basis_hbm,
    spectrum_ref,
    solution_ref,
    residual_ref,
    diag,
    quads,
    right,
    basis,
    basis_hi,
    basis_lo,
    own_quads,
    partner_quads,
    field,
    partner_field,
    partner_basis,
    known,
    partner_known,
    coeffs,
    part,
    plane_in,
    plane_sum,
    ring_in,
    ring_sum,
    gathered,
    load_sems,
    quad_send,
    quad_recv,
    field_send,
    field_recv,
    basis_send,
    basis_recv,
    known_send,
    known_recv,
    sum_send,
    sum_recv,
):
    pt = lax.axis_index("pt")
    sub = lax.axis_index("sub")
    spot = lax.rem(pt, CHIPS)
    core = lax.rem(sub, 2)
    z_hi = lax.div(pt, CHIPS)
    z_lo = lax.div(sub, 2)
    place = spot * 2 + core
    level = z_hi * 4 + z_lo

    def plane_peer(index):
        return (z_hi * CHIPS + lax.div(index, 2), z_lo * 2 + lax.rem(index, 2))

    def ring_peer(index):
        return (lax.div(index, 4) * CHIPS + spot, lax.rem(index, 4) * 2 + core)

    near_role = lax.rem(pt, 2)
    far_role = lax.div(pt, N_PT // 2)
    partners = (
        (pt + 1 - 2 * near_role, sub),
        (lax.rem(pt + N_PT // 2, N_PT), sub),
    )
    roles = (near_role, far_role)

    loads = [
        pltpu.make_async_copy(src, dst, load_sems.at[i])
        for i, (src, dst) in enumerate(
            ((right_hbm, right), (basis_hbm, basis), (quads_hbm, quads), (diag_hbm, diag))
        )
    ]
    for load in loads:
        load.start()

    barrier = pltpu.get_barrier_semaphore()

    def greet_ring(k, carry):
        pl.semaphore_signal(
            barrier, inc=1, device_id=ring_peer(lax.rem(level + k, RING)), device_id_type=MESH
        )
        return carry

    def greet_plane(k, carry):
        pl.semaphore_signal(
            barrier, inc=1, device_id=plane_peer(lax.rem(place + k, PLANE)), device_id_type=MESH
        )
        return carry

    lax.fori_loop(1, RING, greet_ring, 0)
    lax.fori_loop(1, PLANE, greet_plane, 0)

    def put_part(turn, value):
        coeffs[...] = value
        for i in range(PLANE):
            row, lane = 4 * (i % 16), 128 * (i // 16)
            part[turn, i] = coeffs[row : row + 4, lane : lane + 128].astype(PLANE_TYPE)

    def coeff_part(residual):
        high, low = split(residual)
        both = dot_nn(jnp.concatenate([high, low], axis=0), basis_hi[...])
        return both[:RHS] + both[RHS:] + dot_nn(high, basis_lo[...])

    def spread(turn):
        me = part.at[turn]

        def scatter(k, carry):
            peer = lax.rem(place + k, PLANE)
            send(
                me.at[peer],
                plane_in.at[turn, place],
                sum_send.at[turn, 0],
                sum_recv.at[turn, 0],
                plane_peer(peer),
            ).start()
            return carry

        lax.fori_loop(FAR_FIRST, PLANE, scatter, 0)
        lax.fori_loop(1, FAR_FIRST, scatter, 0)
        plane_in[turn, place] = part[turn, place]

    def all_of(ref, count, turn, stage, device):
        span = ref.at[turn, pl.ds(0, count)]
        return send(span, span, sum_send.at[turn, stage], sum_recv.at[turn, stage], device)

    def finish_sum(turn, meanwhile=None):
        all_of(plane_in, PLANE - 1, turn, 0, partners[0]).wait_recv()
        plane_sum[turn] = jnp.sum(plane_in[turn].astype(F32), axis=0).astype(RING_TYPE)

        def along(k, carry):
            send(
                plane_sum.at[turn],
                ring_in.at[turn, level],
                sum_send.at[turn, 1],
                sum_recv.at[turn, 1],
                ring_peer(lax.rem(level + k, RING)),
            ).start()
            return carry

        lax.fori_loop(RING // 2, RING, along, 0)
        lax.fori_loop(1, RING // 2, along, 0)
        ring_in[turn, level] = plane_sum[turn]
        all_of(ring_in, RING - 1, turn, 1, partners[0]).wait_recv()
        ring_sum[turn] = jnp.sum(ring_in[turn].astype(F32), axis=0).astype(GATHER_TYPE)

        def gather(k, carry):
            send(
                ring_sum.at[turn],
                gathered.at[turn, place],
                sum_send.at[turn, 2],
                sum_recv.at[turn, 2],
                plane_peer(lax.rem(place + k, PLANE)),
            ).start()
            return carry

        lax.fori_loop(FAR_FIRST, PLANE, gather, 0)
        lax.fori_loop(1, FAR_FIRST, gather, 0)
        gathered[turn, place] = ring_sum[turn]
        if meanwhile is not None:
            meanwhile()
        all_of(gathered, PLANE - 1, turn, 2, partners[0]).wait_recv()
        for i in range(PLANE):
            row, lane = 4 * (i % 16), 128 * (i // 16)
            coeffs[row : row + 4, lane : lane + 128] = gathered[turn, i].astype(F32)
        return coeffs[...]

    def scaled(summed):
        return split(ROWS / POINTS * spectrum_ref[...] * summed)

    def low_rank(pair, basis_rows):
        both = dot_nt(jnp.concatenate(pair, axis=0), basis_rows)
        return both[:RHS] + both[RHS:]

    def field_copy(m):
        return send(
            field,
            partner_field.at[m],
            field_send.at[m],
            field_recv.at[m],
            partners[m],
        )

    def quad_copy(m):
        return send(
            own_quads.at[m], partner_quads.at[m], quad_send.at[m], quad_recv.at[m], partners[m]
        )

    def basis_copy(m, chunk):
        rows = pl.ds(chunk * CHUNK, CHUNK)
        return send(
            basis_hi.at[rows],
            partner_basis.at[m, rows],
            basis_send.at[m, chunk],
            basis_recv.at[m, chunk],
            partners[m],
        )

    def send_basis(point):
        first = sum(BASIS_AT[:point])
        for chunk in range(first, first + BASIS_AT[point]):
            for m in (1, 0):
                basis_copy(m, chunk).start()

    def known_copy(m):
        return send(known, partner_known.at[m], known_send.at[m], known_recv.at[m], partners[m])

    def put_halves(ref, value):
        ref[0] = value[:, :HALF]
        ref[1] = value[:, HALF:]

    def coupled(m):
        halves = []
        for j in range(2):
            same = j + roles[m] - 2 * j * roles[m]
            other = 1 - same
            halves.append(
                dot_nt(partner_field[m, same], own_quads[m, j])
                + dot_nn(partner_field[m, other], partner_quads[m, other])
            )
        return jnp.concatenate(halves, axis=1)

    loads[0].wait()
    residual = right[...]
    loads[1].wait()
    high, low = split(basis[...])
    basis_hi[...] = high
    basis_lo[...] = low
    put_part(0, coeff_part(residual))
    loads[2].wait()
    for m in range(2):
        for j in range(2):
            keep = mask_ref[m, 0, j].astype(F32)
            rows = quads[m, j * HALF : (j + 1) * HALF, :].astype(F32)
            own_quads[m, j] = (rows * keep).astype(BF16)
    pl.semaphore_wait(barrier, PLANE + RING - 2)

    spread(0)
    for m in (1, 0):
        quad_copy(m).start()
    loads[3].wait()

    centre = 0.5 * (UPPER + LOWER)
    radius = 0.5 * (UPPER - LOWER)
    aspect = centre / radius
    ratio_now = 1.0 / aspect
    ratio_next = 1.0 / (2.0 * aspect - ratio_now)
    gain = 2.0 * ratio_next / radius
    pair = scaled(finish_sum(0, lambda: send_basis(0)))
    term = low_rank(pair, basis_hi[...]) + dot_nt(pair[0], basis_lo[...])
    solution = (0.5 * residual + term) / centre

    direction_bf = solution.astype(BF16)
    put_halves(field, direction_bf)
    for m in (1, 0):
        field_copy(m).start()
    residual = residual - dot_nt(direction_bf, diag[...])
    for m in range(2):
        quad_copy(m).wait_recv()
        field_copy(m).wait_recv()
        residual = residual - coupled(m)

    send_basis(1)
    put_part(1, coeff_part(residual))
    spread(1)
    direction = ratio_next * ratio_now * solution + 0.5 * gain * residual
    known[...] = direction.astype(BF16)
    for m in (1, 0):
        known_copy(m).start()
    for m in range(2):
        field_copy(m).wait_send()
    pair = scaled(finish_sum(1))
    term = low_rank(pair, basis_hi[...]) + dot_nt(pair[0], basis_lo[...])
    direction = direction + gain * term
    solution_ref[...] = solution + direction
    residual = residual - dot_nt(direction.astype(BF16), diag[...])
    for m in range(2):
        for chunk in range(ROWS // CHUNK):
            basis_copy(m, chunk).wait_recv()
        known_copy(m).wait_recv()
        theirs = partner_known[m].astype(F32) + gain * low_rank(pair, partner_basis[m])
        put_halves(partner_field.at[m], theirs.astype(BF16))
        residual = residual - coupled(m)
    residual_ref[...] = residual

    for m in range(2):
        quad_copy(m).wait_send()
        known_copy(m).wait_send()
        for chunk in range(ROWS // CHUNK):
            basis_copy(m, chunk).wait_send()
    for turn in range(ITERS):
        all_of(plane_in, PLANE - 1, turn, 0, partners[0]).wait_send()
        all_of(ring_in, RING - 1, turn, 1, partners[0]).wait_send()
        all_of(gathered, PLANE - 1, turn, 2, partners[0]).wait_send()


def on_device(kernel_diag, pair_quads, tile_mask, right_side, basis, spectrum):
    any_spec = pl.BlockSpec(memory_space=pl.ANY)
    vmem_spec = pl.BlockSpec(memory_space=pltpu.VMEM)
    smem_spec = pl.BlockSpec(memory_space=pltpu.SMEM)
    out = pltpu.VMEM((RHS, ROWS), F32)
    dma = pltpu.SemaphoreType.DMA
    solved, left = pl.pallas_call(
        body,
        name="chebyshev",
        out_shape=(out, out),
        in_specs=[smem_spec, any_spec, any_spec, any_spec, any_spec, vmem_spec],
        out_specs=(vmem_spec, vmem_spec),
        scratch_shapes=[
            pltpu.VMEM((ROWS, ROWS), BF16),
            pltpu.VMEM((2, ROWS, HALF), BF16),
            pltpu.VMEM((RHS, ROWS), F32),
            pltpu.VMEM((ROWS, RANK), F32),
            pltpu.VMEM((ROWS, RANK), BF16),
            pltpu.VMEM((ROWS, RANK), BF16),
            pltpu.VMEM((2, 2, HALF, HALF), BF16),
            pltpu.VMEM((2, 2, HALF, HALF), BF16),
            pltpu.VMEM((2, RHS, HALF), BF16),
            pltpu.VMEM((2, 2, RHS, HALF), BF16),
            pltpu.VMEM((2, ROWS, RANK), BF16),
            pltpu.VMEM((RHS, ROWS), BF16),
            pltpu.VMEM((2, RHS, ROWS), BF16),
            pltpu.VMEM((RHS, RANK), F32),
            pltpu.VMEM((ITERS, PLANE, *PIECE), PLANE_TYPE),
            pltpu.VMEM((ITERS, PLANE, *PIECE), PLANE_TYPE),
            pltpu.VMEM((ITERS, *PIECE), RING_TYPE),
            pltpu.VMEM((ITERS, RING, *PIECE), RING_TYPE),
            pltpu.VMEM((ITERS, *PIECE), GATHER_TYPE),
            pltpu.VMEM((ITERS, PLANE, *PIECE), GATHER_TYPE),
            dma((4,)),
            dma((2,)),
            dma((2,)),
            dma((2,)),
            dma((2,)),
            dma((2, ROWS // CHUNK)),
            dma((2, ROWS // CHUNK)),
            dma((2,)),
            dma((2,)),
            dma((ITERS, 3)),
            dma((ITERS, 3)),
        ],
        compiler_params=pltpu.CompilerParams(collective_id=0, has_side_effects=True),
    )(
        jnp.swapaxes(tile_mask, 1, 2),
        kernel_diag,
        pair_quads,
        right_side.T,
        basis,
        spectrum.reshape(1, RANK),
    )
    return solved.T, left.T


def solution(mesh):
    placed = (
        P(("pt", "sub"), None),
        P(None, ("pt", "sub"), None),
        P(None, ("pt", "sub"), None),
        P(("pt", "sub"), None),
        P(("pt", "sub"), None),
        P(),
    )
    return jax.shard_map(
        on_device,
        mesh=mesh,
        in_specs=placed,
        out_specs=(P(("pt", "sub"), None), P(("pt", "sub"), None)),
        check_vma=False,
    )
```

```python
import jax
import jax.numpy as jnp
from jax import lax
from jax.experimental import pallas as pl
from jax.experimental.pallas import tpu as pltpu
from jax.sharding import PartitionSpec as P

ITERS = 2
LOWER = 0.2
UPPER = 12.0
ROWS = 256
HALF = 128
RHS = 64
RANK = 256
N_PT = 64
N_SUB = 8
POINTS = ROWS * N_PT * N_SUB
PLANE = 32
CHIPS = 16
RING = 16
PIECE = (4, 128)
FAR_FIRST = 12
MESH = pl.DeviceIdType.MESH
F32 = jnp.float32
BF16 = jnp.bfloat16
PLANE_TYPE = BF16
RING_TYPE = BF16
GATHER_TYPE = F32
CHUNK = 32
GROUP = 5
BASIS_AT = (4, 4)


def split(value):
    high = value.astype(BF16)
    return high, (value - high.astype(F32)).astype(BF16)


def dot_nn(left, right):
    return lax.dot_general(left, right, (((1,), (0,)), ((), ())), preferred_element_type=F32)


def dot_nt(left, right):
    return lax.dot_general(left, right, (((1,), (1,)), ((), ())), preferred_element_type=F32)


def each(first, last, action):
    whole = (last - first) // GROUP

    def group(i, carry):
        for j in range(GROUP):
            action(first + i * GROUP + j)
        return carry

    lax.fori_loop(0, whole, group, 0)
    for k in range(first + whole * GROUP, last):
        action(k)


def send(src, dst, send_sem, recv_sem, device):
    return pltpu.make_async_remote_copy(
        src_ref=src,
        dst_ref=dst,
        send_sem=send_sem,
        recv_sem=recv_sem,
        device_id=device,
        device_id_type=MESH,
    )


def body(
    mask_ref,
    diag_hbm,
    quads_hbm,
    right_hbm,
    basis_hbm,
    spectrum_ref,
    solution_ref,
    residual_ref,
    diag,
    quads,
    right,
    basis,
    basis_hi,
    basis_lo,
    own_quads,
    partner_quads,
    field,
    partner_field,
    partner_basis,
    known,
    partner_known,
    coeffs,
    part,
    plane_in,
    plane_sum,
    ring_in,
    ring_sum,
    gathered,
    load_sems,
    quad_send,
    quad_recv,
    field_send,
    field_recv,
    basis_send,
    basis_recv,
    known_send,
    known_recv,
    sum_send,
    sum_recv,
):
    pt = lax.axis_index("pt")
    sub = lax.axis_index("sub")
    spot = lax.rem(pt, CHIPS)
    core = lax.rem(sub, 2)
    z_hi = lax.div(pt, CHIPS)
    z_lo = lax.div(sub, 2)
    place = spot * 2 + core
    level = z_hi * 4 + z_lo

    def plane_peer(index):
        return (z_hi * CHIPS + lax.div(index, 2), z_lo * 2 + lax.rem(index, 2))

    def ring_peer(index):
        return (lax.div(index, 4) * CHIPS + spot, lax.rem(index, 4) * 2 + core)

    near_role = lax.rem(pt, 2)
    far_role = lax.div(pt, N_PT // 2)
    partners = (
        (pt + 1 - 2 * near_role, sub),
        (lax.rem(pt + N_PT // 2, N_PT), sub),
    )
    roles = (near_role, far_role)

    loads = [
        pltpu.make_async_copy(src, dst, load_sems.at[i])
        for i, (src, dst) in enumerate(
            ((right_hbm, right), (basis_hbm, basis), (quads_hbm, quads), (diag_hbm, diag))
        )
    ]
    for load in loads:
        load.start()

    barrier = pltpu.get_barrier_semaphore()

    def greet_ring(k):
        pl.semaphore_signal(
            barrier, inc=1, device_id=ring_peer(lax.rem(level + k, RING)), device_id_type=MESH
        )

    def greet_plane(k):
        pl.semaphore_signal(
            barrier, inc=1, device_id=plane_peer(lax.rem(place + k, PLANE)), device_id_type=MESH
        )

    each(1, RING, greet_ring)
    each(1, PLANE, greet_plane)

    def put_part(turn, value):
        coeffs[...] = value
        for i in range(PLANE):
            row, lane = 4 * (i % 16), 128 * (i // 16)
            part[turn, i] = coeffs[row : row + 4, lane : lane + 128].astype(PLANE_TYPE)

    def coeff_part(residual):
        high, low = split(residual)
        both = dot_nn(jnp.concatenate([high, low], axis=0), basis_hi[...])
        return both[:RHS] + both[RHS:] + dot_nn(high, basis_lo[...])

    def spread(turn):
        me = part.at[turn]

        def scatter(k):
            peer = lax.rem(place + k, PLANE)
            send(
                me.at[peer],
                plane_in.at[turn, place],
                sum_send.at[turn, 0],
                sum_recv.at[turn, 0],
                plane_peer(peer),
            ).start()

        each(FAR_FIRST, PLANE, scatter)
        each(1, FAR_FIRST, scatter)
        plane_in[turn, place] = part[turn, place]

    def all_of(ref, count, turn, stage, device):
        span = ref.at[turn, pl.ds(0, count)]
        return send(span, span, sum_send.at[turn, stage], sum_recv.at[turn, stage], device)

    def finish_sum(turn, beside_ring, beside_gather):
        all_of(plane_in, PLANE - 1, turn, 0, partners[0]).wait_recv()
        plane_sum[turn] = jnp.sum(plane_in[turn].astype(F32), axis=0).astype(RING_TYPE)

        def along(k):
            send(
                plane_sum.at[turn],
                ring_in.at[turn, level],
                sum_send.at[turn, 1],
                sum_recv.at[turn, 1],
                ring_peer(lax.rem(level + k, RING)),
            ).start()

        each(RING // 2, RING, along)
        each(1, RING // 2, along)
        beside_ring()
        ring_in[turn, level] = plane_sum[turn]
        all_of(ring_in, RING - 1, turn, 1, partners[0]).wait_recv()
        ring_sum[turn] = jnp.sum(ring_in[turn].astype(F32), axis=0).astype(GATHER_TYPE)

        def gather(k):
            send(
                ring_sum.at[turn],
                gathered.at[turn, place],
                sum_send.at[turn, 2],
                sum_recv.at[turn, 2],
                plane_peer(lax.rem(place + k, PLANE)),
            ).start()

        each(FAR_FIRST, PLANE, gather)
        each(1, FAR_FIRST, gather)
        gathered[turn, place] = ring_sum[turn]
        beside_gather()
        all_of(gathered, PLANE - 1, turn, 2, partners[0]).wait_recv()
        for i in range(PLANE):
            row, lane = 4 * (i % 16), 128 * (i // 16)
            coeffs[row : row + 4, lane : lane + 128] = gathered[turn, i].astype(F32)
        return coeffs[...]

    def scaled(summed):
        return split(ROWS / POINTS * spectrum_ref[...] * summed)

    def low_rank(pair, basis_rows):
        both = dot_nt(jnp.concatenate(pair, axis=0), basis_rows)
        return both[:RHS] + both[RHS:]

    def field_copy(m):
        return send(
            field,
            partner_field.at[m],
            field_send.at[m],
            field_recv.at[m],
            partners[m],
        )

    def quad_copy(m):
        return send(
            own_quads.at[m], partner_quads.at[m], quad_send.at[m], quad_recv.at[m], partners[m]
        )

    def basis_copy(m, chunk):
        rows = pl.ds(chunk * CHUNK, CHUNK)
        return send(
            basis_hi.at[rows],
            partner_basis.at[m, rows],
            basis_send.at[m, chunk],
            basis_recv.at[m, chunk],
            partners[m],
        )

    def far_basis(point):
        first = sum(BASIS_AT[:point])
        for chunk in range(first, first + BASIS_AT[point]):
            basis_copy(1, chunk).start()

    def near_later():
        known_copy(0).start()
        for chunk in range(ROWS // CHUNK):
            basis_copy(0, chunk).start()

    def known_copy(m):
        return send(known, partner_known.at[m], known_send.at[m], known_recv.at[m], partners[m])

    def put_halves(ref, value):
        ref[0] = value[:, :HALF]
        ref[1] = value[:, HALF:]

    def coupled(m):
        halves = []
        for j in range(2):
            same = j + roles[m] - 2 * j * roles[m]
            other = 1 - same
            halves.append(
                dot_nt(partner_field[m, same], own_quads[m, j])
                + dot_nn(partner_field[m, other], partner_quads[m, other])
            )
        return jnp.concatenate(halves, axis=1)

    loads[0].wait()
    residual = right[...]
    loads[1].wait()
    high, low = split(basis[...])
    basis_hi[...] = high
    basis_lo[...] = low
    put_part(0, coeff_part(residual))
    loads[2].wait()
    for m in range(2):
        for j in range(2):
            keep = mask_ref[m, 0, j].astype(F32)
            rows = quads[m, j * HALF : (j + 1) * HALF, :].astype(F32)
            own_quads[m, j] = (rows * keep).astype(BF16)
    pl.semaphore_wait(barrier, PLANE + RING - 2)

    spread(0)
    quad_copy(1).start()
    loads[3].wait()

    centre = 0.5 * (UPPER + LOWER)
    radius = 0.5 * (UPPER - LOWER)
    aspect = centre / radius
    ratio_now = 1.0 / aspect
    ratio_next = 1.0 / (2.0 * aspect - ratio_now)
    gain = 2.0 * ratio_next / radius
    pair = scaled(finish_sum(0, quad_copy(0).start, lambda: far_basis(0)))
    term = low_rank(pair, basis_hi[...]) + dot_nt(pair[0], basis_lo[...])
    solution = (0.5 * residual + term) / centre

    direction_bf = solution.astype(BF16)
    put_halves(field, direction_bf)
    for m in (1, 0):
        field_copy(m).start()
    residual = residual - dot_nt(direction_bf, diag[...])
    for m in range(2):
        quad_copy(m).wait_recv()
        field_copy(m).wait_recv()
        residual = residual - coupled(m)

    far_basis(1)
    put_part(1, coeff_part(residual))
    spread(1)
    direction = ratio_next * ratio_now * solution + 0.5 * gain * residual
    known[...] = direction.astype(BF16)
    known_copy(1).start()
    for m in range(2):
        field_copy(m).wait_send()
    pair = scaled(finish_sum(1, near_later, lambda: None))
    term = low_rank(pair, basis_hi[...]) + dot_nt(pair[0], basis_lo[...])
    direction = direction + gain * term
    solution_ref[...] = solution + direction
    residual = residual - dot_nt(direction.astype(BF16), diag[...])
    for m in range(2):
        for chunk in range(ROWS // CHUNK):
            basis_copy(m, chunk).wait_recv()
        known_copy(m).wait_recv()
        theirs = partner_known[m].astype(F32) + gain * low_rank(pair, partner_basis[m])
        put_halves(partner_field.at[m], theirs.astype(BF16))
        residual = residual - coupled(m)
    residual_ref[...] = residual

    for m in range(2):
        quad_copy(m).wait_send()
        known_copy(m).wait_send()
        for chunk in range(ROWS // CHUNK):
            basis_copy(m, chunk).wait_send()
    for turn in range(ITERS):
        all_of(plane_in, PLANE - 1, turn, 0, partners[0]).wait_send()
        all_of(ring_in, RING - 1, turn, 1, partners[0]).wait_send()
        all_of(gathered, PLANE - 1, turn, 2, partners[0]).wait_send()


def on_device(kernel_diag, pair_quads, tile_mask, right_side, basis, spectrum):
    any_spec = pl.BlockSpec(memory_space=pl.ANY)
    vmem_spec = pl.BlockSpec(memory_space=pltpu.VMEM)
    smem_spec = pl.BlockSpec(memory_space=pltpu.SMEM)
    out = pltpu.VMEM((RHS, ROWS), F32)
    dma = pltpu.SemaphoreType.DMA
    solved, left = pl.pallas_call(
        body,
        name="chebyshev",
        out_shape=(out, out),
        in_specs=[smem_spec, any_spec, any_spec, any_spec, any_spec, vmem_spec],
        out_specs=(vmem_spec, vmem_spec),
        scratch_shapes=[
            pltpu.VMEM((ROWS, ROWS), BF16),
            pltpu.VMEM((2, ROWS, HALF), BF16),
            pltpu.VMEM((RHS, ROWS), F32),
            pltpu.VMEM((ROWS, RANK), F32),
            pltpu.VMEM((ROWS, RANK), BF16),
            pltpu.VMEM((ROWS, RANK), BF16),
            pltpu.VMEM((2, 2, HALF, HALF), BF16),
            pltpu.VMEM((2, 2, HALF, HALF), BF16),
            pltpu.VMEM((2, RHS, HALF), BF16),
            pltpu.VMEM((2, 2, RHS, HALF), BF16),
            pltpu.VMEM((2, ROWS, RANK), BF16),
            pltpu.VMEM((RHS, ROWS), BF16),
            pltpu.VMEM((2, RHS, ROWS), BF16),
            pltpu.VMEM((RHS, RANK), F32),
            pltpu.VMEM((ITERS, PLANE, *PIECE), PLANE_TYPE),
            pltpu.VMEM((ITERS, PLANE, *PIECE), PLANE_TYPE),
            pltpu.VMEM((ITERS, *PIECE), RING_TYPE),
            pltpu.VMEM((ITERS, RING, *PIECE), RING_TYPE),
            pltpu.VMEM((ITERS, *PIECE), GATHER_TYPE),
            pltpu.VMEM((ITERS, PLANE, *PIECE), GATHER_TYPE),
            dma((4,)),
            dma((2,)),
            dma((2,)),
            dma((2,)),
            dma((2,)),
            dma((2, ROWS // CHUNK)),
            dma((2, ROWS // CHUNK)),
            dma((2,)),
            dma((2,)),
            dma((ITERS, 3)),
            dma((ITERS, 3)),
        ],
        compiler_params=pltpu.CompilerParams(collective_id=0, has_side_effects=True),
    )(
        jnp.swapaxes(tile_mask, 1, 2),
        kernel_diag,
        pair_quads,
        right_side.T,
        basis,
        spectrum.reshape(1, RANK),
    )
    return solved.T, left.T


def solution(mesh):
    placed = (
        P(("pt", "sub"), None),
        P(None, ("pt", "sub"), None),
        P(None, ("pt", "sub"), None),
        P(("pt", "sub"), None),
        P(("pt", "sub"), None),
        P(),
    )
    return jax.shard_map(
        on_device,
        mesh=mesh,
        in_specs=placed,
        out_specs=(P(("pt", "sub"), None), P(("pt", "sub"), None)),
        check_vma=False,
    )
```

```python
import jax
import jax.numpy as jnp
from jax import lax
from jax.experimental import pallas as pl
from jax.experimental.pallas import tpu as pltpu
from jax.sharding import PartitionSpec as P

ITERS = 2
LOWER = 0.2
UPPER = 12.0
ROWS = 256
HALF = 128
RHS = 64
RANK = 256
N_PT = 64
N_SUB = 8
POINTS = ROWS * N_PT * N_SUB
PLANE = 32
CHIPS = 16
RING = 16
PIECE = (4, 128)
FAR_FIRST = 12
MESH = pl.DeviceIdType.MESH
F32 = jnp.float32
BF16 = jnp.bfloat16
PLANE_TYPE = BF16
RING_TYPE = BF16
GATHER_TYPE = F32
CHUNK = 32
GROUP = 5
BASIS_AT = (4, 1, 3)


def split(value):
    high = value.astype(BF16)
    return high, (value - high.astype(F32)).astype(BF16)


def dot_nn(left, right):
    return lax.dot_general(left, right, (((1,), (0,)), ((), ())), preferred_element_type=F32)


def dot_nt(left, right):
    return lax.dot_general(left, right, (((1,), (1,)), ((), ())), preferred_element_type=F32)


def each(first, last, action):
    whole = (last - first) // GROUP

    def group(i, carry):
        for j in range(GROUP):
            action(first + i * GROUP + j)
        return carry

    lax.fori_loop(0, whole, group, 0)
    for k in range(first + whole * GROUP, last):
        action(k)


def send(src, dst, send_sem, recv_sem, device):
    return pltpu.make_async_remote_copy(
        src_ref=src,
        dst_ref=dst,
        send_sem=send_sem,
        recv_sem=recv_sem,
        device_id=device,
        device_id_type=MESH,
    )


def body(
    mask_ref,
    diag_hbm,
    quads_hbm,
    right_hbm,
    basis_hbm,
    spectrum_ref,
    solution_ref,
    residual_ref,
    diag,
    quads,
    right,
    basis,
    basis_hi,
    basis_lo,
    own_quads,
    partner_quads,
    field,
    partner_field,
    partner_basis,
    known,
    partner_known,
    coeffs,
    part,
    plane_in,
    plane_sum,
    ring_in,
    ring_sum,
    gathered,
    load_sems,
    quad_send,
    quad_recv,
    field_send,
    field_recv,
    basis_send,
    basis_recv,
    known_send,
    known_recv,
    sum_send,
    sum_recv,
):
    pt = lax.axis_index("pt")
    sub = lax.axis_index("sub")
    spot = lax.rem(pt, CHIPS)
    core = lax.rem(sub, 2)
    z_hi = lax.div(pt, CHIPS)
    z_lo = lax.div(sub, 2)
    place = spot * 2 + core
    level = z_hi * 4 + z_lo

    def plane_peer(index):
        return (z_hi * CHIPS + lax.div(index, 2), z_lo * 2 + lax.rem(index, 2))

    def ring_peer(index):
        return (lax.div(index, 4) * CHIPS + spot, lax.rem(index, 4) * 2 + core)

    near_role = lax.rem(pt, 2)
    far_role = lax.div(pt, N_PT // 2)
    partners = (
        (pt + 1 - 2 * near_role, sub),
        (lax.rem(pt + N_PT // 2, N_PT), sub),
    )
    roles = (near_role, far_role)

    loads = [
        pltpu.make_async_copy(src, dst, load_sems.at[i])
        for i, (src, dst) in enumerate(
            ((right_hbm, right), (basis_hbm, basis), (quads_hbm, quads), (diag_hbm, diag))
        )
    ]
    for load in loads:
        load.start()

    barrier = pltpu.get_barrier_semaphore()

    def greet_ring(k):
        pl.semaphore_signal(
            barrier, inc=1, device_id=ring_peer(lax.rem(level + k, RING)), device_id_type=MESH
        )

    def greet_plane(k):
        pl.semaphore_signal(
            barrier, inc=1, device_id=plane_peer(lax.rem(place + k, PLANE)), device_id_type=MESH
        )

    each(1, RING, greet_ring)
    each(1, PLANE, greet_plane)

    def put_part(turn, value):
        coeffs[...] = value
        for i in range(PLANE):
            row, lane = 4 * (i % 16), 128 * (i // 16)
            part[turn, i] = coeffs[row : row + 4, lane : lane + 128].astype(PLANE_TYPE)

    def coeff_part(residual):
        high, low = split(residual)
        both = dot_nn(jnp.concatenate([high, low], axis=0), basis_hi[...])
        return both[:RHS] + both[RHS:] + dot_nn(high, basis_lo[...])

    def spread(turn):
        me = part.at[turn]

        def scatter(k):
            peer = lax.rem(place + k, PLANE)
            send(
                me.at[peer],
                plane_in.at[turn, place],
                sum_send.at[turn, 0],
                sum_recv.at[turn, 0],
                plane_peer(peer),
            ).start()

        each(FAR_FIRST, PLANE, scatter)
        each(1, FAR_FIRST, scatter)
        plane_in[turn, place] = part[turn, place]

    def all_of(ref, count, turn, stage, device):
        span = ref.at[turn, pl.ds(0, count)]
        return send(span, span, sum_send.at[turn, stage], sum_recv.at[turn, stage], device)

    def finish_sum(turn, beside_ring, beside_gather):
        all_of(plane_in, PLANE - 1, turn, 0, partners[0]).wait_recv()
        plane_sum[turn] = jnp.sum(plane_in[turn].astype(F32), axis=0).astype(RING_TYPE)

        def along(k):
            send(
                plane_sum.at[turn],
                ring_in.at[turn, level],
                sum_send.at[turn, 1],
                sum_recv.at[turn, 1],
                ring_peer(lax.rem(level + k, RING)),
            ).start()

        each(RING // 2, RING, along)
        each(1, RING // 2, along)
        beside_ring()
        ring_in[turn, level] = plane_sum[turn]
        all_of(ring_in, RING - 1, turn, 1, partners[0]).wait_recv()
        ring_sum[turn] = jnp.sum(ring_in[turn].astype(F32), axis=0).astype(GATHER_TYPE)

        def gather(k):
            send(
                ring_sum.at[turn],
                gathered.at[turn, place],
                sum_send.at[turn, 2],
                sum_recv.at[turn, 2],
                plane_peer(lax.rem(place + k, PLANE)),
            ).start()

        each(FAR_FIRST, PLANE, gather)
        each(1, FAR_FIRST, gather)
        gathered[turn, place] = ring_sum[turn]
        beside_gather()
        all_of(gathered, PLANE - 1, turn, 2, partners[0]).wait_recv()
        for i in range(PLANE):
            row, lane = 4 * (i % 16), 128 * (i // 16)
            coeffs[row : row + 4, lane : lane + 128] = gathered[turn, i].astype(F32)
        return coeffs[...]

    def scaled(summed):
        return split(ROWS / POINTS * spectrum_ref[...] * summed)

    def low_rank(pair, basis_rows):
        both = dot_nt(jnp.concatenate(pair, axis=0), basis_rows)
        return both[:RHS] + both[RHS:]

    def field_copy(m):
        return send(
            field,
            partner_field.at[m],
            field_send.at[m],
            field_recv.at[m],
            partners[m],
        )

    def quad_copy(m):
        return send(
            own_quads.at[m], partner_quads.at[m], quad_send.at[m], quad_recv.at[m], partners[m]
        )

    def basis_copy(m, chunk):
        rows = pl.ds(chunk * CHUNK, CHUNK)
        return send(
            basis_hi.at[rows],
            partner_basis.at[m, rows],
            basis_send.at[m, chunk],
            basis_recv.at[m, chunk],
            partners[m],
        )

    def far_basis(point):
        first = sum(BASIS_AT[:point])
        for chunk in range(first, first + BASIS_AT[point]):
            basis_copy(1, chunk).start()

    def near_later():
        known_copy(0).start()
        for chunk in range(ROWS // CHUNK):
            basis_copy(0, chunk).start()

    def known_copy(m):
        return send(known, partner_known.at[m], known_send.at[m], known_recv.at[m], partners[m])

    def put_halves(ref, value):
        ref[0] = value[:, :HALF]
        ref[1] = value[:, HALF:]

    def coupled(m):
        halves = []
        for j in range(2):
            same = j + roles[m] - 2 * j * roles[m]
            other = 1 - same
            halves.append(
                dot_nt(partner_field[m, same], own_quads[m, j])
                + dot_nn(partner_field[m, other], partner_quads[m, other])
            )
        return jnp.concatenate(halves, axis=1)

    loads[0].wait()
    residual = right[...]
    loads[1].wait()
    high, low = split(basis[...])
    basis_hi[...] = high
    basis_lo[...] = low
    put_part(0, coeff_part(residual))
    loads[2].wait()
    for m in range(2):
        for j in range(2):
            keep = mask_ref[m, 0, j].astype(F32)
            rows = quads[m, j * HALF : (j + 1) * HALF, :].astype(F32)
            own_quads[m, j] = (rows * keep).astype(BF16)
    pl.semaphore_wait(barrier, PLANE + RING - 2)

    spread(0)
    quad_copy(1).start()
    loads[3].wait()

    centre = 0.5 * (UPPER + LOWER)
    radius = 0.5 * (UPPER - LOWER)
    aspect = centre / radius
    ratio_now = 1.0 / aspect
    ratio_next = 1.0 / (2.0 * aspect - ratio_now)
    gain = 2.0 * ratio_next / radius
    pair = scaled(finish_sum(0, quad_copy(0).start, lambda: far_basis(0)))
    term = low_rank(pair, basis_hi[...]) + dot_nt(pair[0], basis_lo[...])
    solution = (0.5 * residual + term) / centre

    direction_bf = solution.astype(BF16)
    put_halves(field, direction_bf)
    for m in (1, 0):
        field_copy(m).start()
    far_basis(1)
    residual = residual - dot_nt(direction_bf, diag[...])
    for m in range(2):
        quad_copy(m).wait_recv()
        field_copy(m).wait_recv()
        residual = residual - coupled(m)

    far_basis(2)
    put_part(1, coeff_part(residual))
    spread(1)
    direction = ratio_next * ratio_now * solution + 0.5 * gain * residual
    known[...] = direction.astype(BF16)
    known_copy(1).start()
    for m in range(2):
        field_copy(m).wait_send()
    pair = scaled(finish_sum(1, near_later, lambda: None))
    term = low_rank(pair, basis_hi[...]) + dot_nt(pair[0], basis_lo[...])
    direction = direction + gain * term
    solution_ref[...] = solution + direction
    residual = residual - dot_nt(direction.astype(BF16), diag[...])
    for m in range(2):
        for chunk in range(ROWS // CHUNK):
            basis_copy(m, chunk).wait_recv()
        known_copy(m).wait_recv()
        theirs = partner_known[m].astype(F32) + gain * low_rank(pair, partner_basis[m])
        put_halves(partner_field.at[m], theirs.astype(BF16))
        residual = residual - coupled(m)
    residual_ref[...] = residual

    for m in range(2):
        quad_copy(m).wait_send()
        known_copy(m).wait_send()
        for chunk in range(ROWS // CHUNK):
            basis_copy(m, chunk).wait_send()
    for turn in range(ITERS):
        all_of(plane_in, PLANE - 1, turn, 0, partners[0]).wait_send()
        all_of(ring_in, RING - 1, turn, 1, partners[0]).wait_send()
        all_of(gathered, PLANE - 1, turn, 2, partners[0]).wait_send()


def on_device(kernel_diag, pair_quads, tile_mask, right_side, basis, spectrum):
    any_spec = pl.BlockSpec(memory_space=pl.ANY)
    vmem_spec = pl.BlockSpec(memory_space=pltpu.VMEM)
    smem_spec = pl.BlockSpec(memory_space=pltpu.SMEM)
    out = pltpu.VMEM((RHS, ROWS), F32)
    dma = pltpu.SemaphoreType.DMA
    solved, left = pl.pallas_call(
        body,
        name="chebyshev",
        out_shape=(out, out),
        in_specs=[smem_spec, any_spec, any_spec, any_spec, any_spec, vmem_spec],
        out_specs=(vmem_spec, vmem_spec),
        scratch_shapes=[
            pltpu.VMEM((ROWS, ROWS), BF16),
            pltpu.VMEM((2, ROWS, HALF), BF16),
            pltpu.VMEM((RHS, ROWS), F32),
            pltpu.VMEM((ROWS, RANK), F32),
            pltpu.VMEM((ROWS, RANK), BF16),
            pltpu.VMEM((ROWS, RANK), BF16),
            pltpu.VMEM((2, 2, HALF, HALF), BF16),
            pltpu.VMEM((2, 2, HALF, HALF), BF16),
            pltpu.VMEM((2, RHS, HALF), BF16),
            pltpu.VMEM((2, 2, RHS, HALF), BF16),
            pltpu.VMEM((2, ROWS, RANK), BF16),
            pltpu.VMEM((RHS, ROWS), BF16),
            pltpu.VMEM((2, RHS, ROWS), BF16),
            pltpu.VMEM((RHS, RANK), F32),
            pltpu.VMEM((ITERS, PLANE, *PIECE), PLANE_TYPE),
            pltpu.VMEM((ITERS, PLANE, *PIECE), PLANE_TYPE),
            pltpu.VMEM((ITERS, *PIECE), RING_TYPE),
            pltpu.VMEM((ITERS, RING, *PIECE), RING_TYPE),
            pltpu.VMEM((ITERS, *PIECE), GATHER_TYPE),
            pltpu.VMEM((ITERS, PLANE, *PIECE), GATHER_TYPE),
            dma((4,)),
            dma((2,)),
            dma((2,)),
            dma((2,)),
            dma((2,)),
            dma((2, ROWS // CHUNK)),
            dma((2, ROWS // CHUNK)),
            dma((2,)),
            dma((2,)),
            dma((ITERS, 3)),
            dma((ITERS, 3)),
        ],
        compiler_params=pltpu.CompilerParams(collective_id=0, has_side_effects=True),
    )(
        jnp.swapaxes(tile_mask, 1, 2),
        kernel_diag,
        pair_quads,
        right_side.T,
        basis,
        spectrum.reshape(1, RANK),
    )
    return solved.T, left.T


def solution(mesh):
    placed = (
        P(("pt", "sub"), None),
        P(None, ("pt", "sub"), None),
        P(None, ("pt", "sub"), None),
        P(("pt", "sub"), None),
        P(("pt", "sub"), None),
        P(),
    )
    return jax.shard_map(
        on_device,
        mesh=mesh,
        in_specs=placed,
        out_specs=(P(("pt", "sub"), None), P(("pt", "sub"), None)),
        check_vma=False,
    )
```

```python
import jax
import jax.numpy as jnp
from jax import lax
from jax.experimental import pallas as pl
from jax.experimental.pallas import tpu as pltpu
from jax.sharding import PartitionSpec as P

ITERS = 2
LOWER = 0.2
UPPER = 12.0
ROWS = 256
HALF = 128
RHS = 64
RANK = 256
N_PT = 64
N_SUB = 8
POINTS = ROWS * N_PT * N_SUB
PLANE = 32
CHIPS = 16
RING = 16
PIECE = (4, 128)
FAR_FIRST = 12
MESH = pl.DeviceIdType.MESH
F32 = jnp.float32
BF16 = jnp.bfloat16
PLANE_TYPE = BF16
RING_TYPE = BF16
GATHER_TYPE = F32
CHUNK = 32
GROUP = 5
BASIS_AT = (4, 1, 3)


def split(value):
    high = value.astype(BF16)
    return high, (value - high.astype(F32)).astype(BF16)


def dot_nn(left, right):
    return lax.dot_general(left, right, (((1,), (0,)), ((), ())), preferred_element_type=F32)


def dot_nt(left, right):
    return lax.dot_general(left, right, (((1,), (1,)), ((), ())), preferred_element_type=F32)


def each(first, last, action):
    whole = (last - first) // GROUP

    def group(i, carry):
        for j in range(GROUP):
            action(first + i * GROUP + j)
        return carry

    lax.fori_loop(0, whole, group, 0)
    for k in range(first + whole * GROUP, last):
        action(k)


def send(src, dst, send_sem, recv_sem, device):
    return pltpu.make_async_remote_copy(
        src_ref=src,
        dst_ref=dst,
        send_sem=send_sem,
        recv_sem=recv_sem,
        device_id=device,
        device_id_type=MESH,
    )


def body(
    mask_hbm,
    diag_hbm,
    quads_hbm,
    right_hbm,
    basis_hbm,
    spectrum_hbm,
    solution_ref,
    residual_ref,
    mask_ref,
    spectrum_ref,
    diag,
    quads,
    right,
    basis,
    basis_hi,
    basis_lo,
    own_quads,
    partner_quads,
    field,
    partner_field,
    partner_basis,
    known,
    partner_known,
    coeffs,
    part,
    plane_in,
    plane_sum,
    ring_in,
    ring_sum,
    gathered,
    load_sems,
    quad_send,
    quad_recv,
    field_send,
    field_recv,
    basis_send,
    basis_recv,
    known_send,
    known_recv,
    sum_send,
    sum_recv,
):
    pt = lax.axis_index("pt")
    sub = lax.axis_index("sub")
    spot = lax.rem(pt, CHIPS)
    core = lax.rem(sub, 2)
    z_hi = lax.div(pt, CHIPS)
    z_lo = lax.div(sub, 2)
    place = spot * 2 + core
    level = z_hi * 4 + z_lo

    def plane_peer(index):
        return (z_hi * CHIPS + lax.div(index, 2), z_lo * 2 + lax.rem(index, 2))

    def ring_peer(index):
        return (lax.div(index, 4) * CHIPS + spot, lax.rem(index, 4) * 2 + core)

    near_role = lax.rem(pt, 2)
    far_role = lax.div(pt, N_PT // 2)
    partners = (
        (pt + 1 - 2 * near_role, sub),
        (lax.rem(pt + N_PT // 2, N_PT), sub),
    )
    roles = (near_role, far_role)

    loads = [
        pltpu.make_async_copy(src, dst, load_sems.at[i])
        for i, (src, dst) in enumerate(
            (
                (right_hbm, right),
                (basis_hbm, basis),
                (quads_hbm, quads),
                (mask_hbm, mask_ref),
                (diag_hbm, diag),
                (spectrum_hbm, spectrum_ref),
            )
        )
    ]
    for load in loads:
        load.start()

    barrier = pltpu.get_barrier_semaphore()

    def greet_ring(k):
        pl.semaphore_signal(
            barrier, inc=1, device_id=ring_peer(lax.rem(level + k, RING)), device_id_type=MESH
        )

    def greet_plane(k):
        pl.semaphore_signal(
            barrier, inc=1, device_id=plane_peer(lax.rem(place + k, PLANE)), device_id_type=MESH
        )

    each(1, RING, greet_ring)
    each(1, PLANE, greet_plane)

    def put_part(turn, value):
        coeffs[...] = value
        for i in range(PLANE):
            row, lane = 4 * (i % 16), 128 * (i // 16)
            part[turn, i] = coeffs[row : row + 4, lane : lane + 128].astype(PLANE_TYPE)

    def coeff_part(residual):
        high, low = split(residual)
        both = dot_nn(jnp.concatenate([high, low], axis=0), basis_hi[...])
        return both[:RHS] + both[RHS:] + dot_nn(high, basis_lo[...])

    def spread(turn):
        me = part.at[turn]

        def scatter(k):
            peer = lax.rem(place + k, PLANE)
            send(
                me.at[peer],
                plane_in.at[turn, place],
                sum_send.at[turn, 0],
                sum_recv.at[turn, 0],
                plane_peer(peer),
            ).start()

        each(FAR_FIRST, PLANE, scatter)
        each(1, FAR_FIRST, scatter)
        plane_in[turn, place] = part[turn, place]

    def all_of(ref, count, turn, stage, device):
        span = ref.at[turn, pl.ds(0, count)]
        return send(span, span, sum_send.at[turn, stage], sum_recv.at[turn, stage], device)

    def finish_sum(turn, beside_ring, beside_gather):
        all_of(plane_in, PLANE - 1, turn, 0, partners[0]).wait_recv()
        plane_sum[turn] = jnp.sum(plane_in[turn].astype(F32), axis=0).astype(RING_TYPE)

        def along(k):
            send(
                plane_sum.at[turn],
                ring_in.at[turn, level],
                sum_send.at[turn, 1],
                sum_recv.at[turn, 1],
                ring_peer(lax.rem(level + k, RING)),
            ).start()

        each(RING // 2, RING, along)
        each(1, RING // 2, along)
        beside_ring()
        ring_in[turn, level] = plane_sum[turn]
        all_of(ring_in, RING - 1, turn, 1, partners[0]).wait_recv()
        ring_sum[turn] = jnp.sum(ring_in[turn].astype(F32), axis=0).astype(GATHER_TYPE)

        def gather(k):
            send(
                ring_sum.at[turn],
                gathered.at[turn, place],
                sum_send.at[turn, 2],
                sum_recv.at[turn, 2],
                plane_peer(lax.rem(place + k, PLANE)),
            ).start()

        each(FAR_FIRST, PLANE, gather)
        each(1, FAR_FIRST, gather)
        gathered[turn, place] = ring_sum[turn]
        beside_gather()
        all_of(gathered, PLANE - 1, turn, 2, partners[0]).wait_recv()
        for i in range(PLANE):
            row, lane = 4 * (i % 16), 128 * (i // 16)
            coeffs[row : row + 4, lane : lane + 128] = gathered[turn, i].astype(F32)
        return coeffs[...]

    def scaled(summed):
        return split(ROWS / POINTS * spectrum_ref[...] * summed)

    def low_rank(pair, basis_rows):
        both = dot_nt(jnp.concatenate(pair, axis=0), basis_rows)
        return both[:RHS] + both[RHS:]

    def field_copy(m):
        return send(
            field,
            partner_field.at[m],
            field_send.at[m],
            field_recv.at[m],
            partners[m],
        )

    def quad_copy(m):
        return send(
            own_quads.at[m], partner_quads.at[m], quad_send.at[m], quad_recv.at[m], partners[m]
        )

    def basis_copy(m, chunk):
        rows = pl.ds(chunk * CHUNK, CHUNK)
        return send(
            basis_hi.at[rows],
            partner_basis.at[m, rows],
            basis_send.at[m, chunk],
            basis_recv.at[m, chunk],
            partners[m],
        )

    def far_basis(point):
        first = sum(BASIS_AT[:point])
        for chunk in range(first, first + BASIS_AT[point]):
            basis_copy(1, chunk).start()

    def near_later():
        known_copy(0).start()
        for chunk in range(ROWS // CHUNK):
            basis_copy(0, chunk).start()

    def known_copy(m):
        return send(known, partner_known.at[m], known_send.at[m], known_recv.at[m], partners[m])

    def put_halves(ref, value):
        ref[0] = value[:, :HALF]
        ref[1] = value[:, HALF:]

    def coupled(m):
        halves = []
        for j in range(2):
            same = j + roles[m] - 2 * j * roles[m]
            other = 1 - same
            halves.append(
                dot_nt(partner_field[m, same], own_quads[m, j])
                + dot_nn(partner_field[m, other], partner_quads[m, other])
            )
        return jnp.concatenate(halves, axis=1)

    loads[0].wait()
    residual = right[...]
    loads[1].wait()
    high, low = split(basis[...])
    basis_hi[...] = high
    basis_lo[...] = low
    put_part(0, coeff_part(residual))
    loads[2].wait()
    loads[3].wait()
    for m in range(2):
        for j in range(2):
            keep = mask_ref[m, 0, j].astype(F32)
            rows = quads[m, j * HALF : (j + 1) * HALF, :].astype(F32)
            own_quads[m, j] = (rows * keep).astype(BF16)
    pl.semaphore_wait(barrier, PLANE + RING - 2)

    spread(0)
    quad_copy(1).start()
    loads[4].wait()
    loads[5].wait()

    centre = 0.5 * (UPPER + LOWER)
    radius = 0.5 * (UPPER - LOWER)
    aspect = centre / radius
    ratio_now = 1.0 / aspect
    ratio_next = 1.0 / (2.0 * aspect - ratio_now)
    gain = 2.0 * ratio_next / radius
    pair = scaled(finish_sum(0, quad_copy(0).start, lambda: far_basis(0)))
    term = low_rank(pair, basis_hi[...]) + dot_nt(pair[0], basis_lo[...])
    solution = (0.5 * residual + term) / centre

    direction_bf = solution.astype(BF16)
    put_halves(field, direction_bf)
    for m in (1, 0):
        field_copy(m).start()
    far_basis(1)
    residual = residual - dot_nt(direction_bf, diag[...])
    for m in range(2):
        quad_copy(m).wait_recv()
        field_copy(m).wait_recv()
        residual = residual - coupled(m)

    far_basis(2)
    put_part(1, coeff_part(residual))
    spread(1)
    direction = ratio_next * ratio_now * solution + 0.5 * gain * residual
    known[...] = direction.astype(BF16)
    known_copy(1).start()
    for m in range(2):
        field_copy(m).wait_send()
    pair = scaled(finish_sum(1, near_later, lambda: None))
    term = low_rank(pair, basis_hi[...]) + dot_nt(pair[0], basis_lo[...])
    direction = direction + gain * term
    solution_ref[...] = solution + direction
    residual = residual - dot_nt(direction.astype(BF16), diag[...])
    for m in range(2):
        for chunk in range(ROWS // CHUNK):
            basis_copy(m, chunk).wait_recv()
        known_copy(m).wait_recv()
        theirs = partner_known[m].astype(F32) + gain * low_rank(pair, partner_basis[m])
        put_halves(partner_field.at[m], theirs.astype(BF16))
        residual = residual - coupled(m)
    residual_ref[...] = residual

    for m in range(2):
        quad_copy(m).wait_send()
        known_copy(m).wait_send()
        for chunk in range(ROWS // CHUNK):
            basis_copy(m, chunk).wait_send()
    for turn in range(ITERS):
        all_of(plane_in, PLANE - 1, turn, 0, partners[0]).wait_send()
        all_of(ring_in, RING - 1, turn, 1, partners[0]).wait_send()
        all_of(gathered, PLANE - 1, turn, 2, partners[0]).wait_send()


def on_device(kernel_diag, pair_quads, tile_mask, right_side, basis, spectrum):
    any_spec = pl.BlockSpec(memory_space=pl.ANY)
    vmem_spec = pl.BlockSpec(memory_space=pltpu.VMEM)
    out = pltpu.VMEM((RHS, ROWS), F32)
    dma = pltpu.SemaphoreType.DMA
    solved, left = pl.pallas_call(
        body,
        name="chebyshev",
        out_shape=(out, out),
        in_specs=[any_spec] * 6,
        out_specs=(vmem_spec, vmem_spec),
        scratch_shapes=[
            pltpu.SMEM((2, 1, 2), jnp.int32),
            pltpu.VMEM((1, RANK), F32),
            pltpu.VMEM((ROWS, ROWS), BF16),
            pltpu.VMEM((2, ROWS, HALF), BF16),
            pltpu.VMEM((RHS, ROWS), F32),
            pltpu.VMEM((ROWS, RANK), F32),
            pltpu.VMEM((ROWS, RANK), BF16),
            pltpu.VMEM((ROWS, RANK), BF16),
            pltpu.VMEM((2, 2, HALF, HALF), BF16),
            pltpu.VMEM((2, 2, HALF, HALF), BF16),
            pltpu.VMEM((2, RHS, HALF), BF16),
            pltpu.VMEM((2, 2, RHS, HALF), BF16),
            pltpu.VMEM((2, ROWS, RANK), BF16),
            pltpu.VMEM((RHS, ROWS), BF16),
            pltpu.VMEM((2, RHS, ROWS), BF16),
            pltpu.VMEM((RHS, RANK), F32),
            pltpu.VMEM((ITERS, PLANE, *PIECE), PLANE_TYPE),
            pltpu.VMEM((ITERS, PLANE, *PIECE), PLANE_TYPE),
            pltpu.VMEM((ITERS, *PIECE), RING_TYPE),
            pltpu.VMEM((ITERS, RING, *PIECE), RING_TYPE),
            pltpu.VMEM((ITERS, *PIECE), GATHER_TYPE),
            pltpu.VMEM((ITERS, PLANE, *PIECE), GATHER_TYPE),
            dma((6,)),
            dma((2,)),
            dma((2,)),
            dma((2,)),
            dma((2,)),
            dma((2, ROWS // CHUNK)),
            dma((2, ROWS // CHUNK)),
            dma((2,)),
            dma((2,)),
            dma((ITERS, 3)),
            dma((ITERS, 3)),
        ],
        compiler_params=pltpu.CompilerParams(collective_id=0, has_side_effects=True),
    )(
        jnp.swapaxes(tile_mask, 1, 2),
        kernel_diag,
        pair_quads,
        right_side.T,
        basis,
        spectrum.reshape(1, RANK),
    )
    return solved.T, left.T


def solution(mesh):
    placed = (
        P(("pt", "sub"), None),
        P(None, ("pt", "sub"), None),
        P(None, ("pt", "sub"), None),
        P(("pt", "sub"), None),
        P(("pt", "sub"), None),
        P(),
    )
    return jax.shard_map(
        on_device,
        mesh=mesh,
        in_specs=placed,
        out_specs=(P(("pt", "sub"), None), P(("pt", "sub"), None)),
        check_vma=False,
    )
```
